256 devices in a mesh: line: 8 (over z_lo, core), bus: 32 (over y, x, z_hi).
Axes of the slice: x: 4, y: 4, z: 8 (z_hi: 2, z_lo: 4; z = z_hi * 4 + z_lo), core: 2. Of those that a mesh axis runs over, the one named last changes fastest.
Arguments:
- injections: float32 [64, 69632], P(None, 'bus'), may hold values from -6 to 6
- transfer_factors: float32 [4096, 69632], P('line', 'bus'), may hold values from -0.0234375 to 0.0234375
- outage_factors: float32 [4096, 8192], P('line', 'bus'), may hold values from -1 to 1
- outage_line: int32 [8192], P('bus'), may hold values from 0 to 4095
- limit_table: int32 [4, 4096], P(None, 'line'), may hold values from 1 to 4
- scenario_tier: int32 [64], replicated, may hold values from 0 to 3
Outputs:
- injection_grad: float32 [64, 69632], P('line', 'bus')
- mean_penalty: float32 [64], replicated
The draws below stay inside these ranges and needn't reach their ends.
All inputs are finite; a program needn't handle non-finite values.
Results may differ from the reference program's by a relative error of at most 0.0003.
Values sent between devices are 32-bit elements; how exact they have to be, the bound alone decides.
A program may use at most 64 MiB of HBM per device.

```python
import jax
import jax.numpy as jnp
from jax import lax

BUSES = 69632
LINES = 4096
OUTAGES = 8192
TIERS = 4
SCEN = 64


def with_ends(array, rng, least, high):
    longest = array.shape.index(max(array.shape))
    spots = []
    for shift in (0, 1):
        where = [jax.random.randint(jax.random.fold_in(rng, axis), (), 0, length) for axis, length in enumerate(array.shape)]
        where[longest] = (where[longest] + shift) % array.shape[longest]
        spots.append(tuple(where))
    return array.at[spots[0]].set(least).at[spots[1]].set(high)


def levels(stream_key, extent, shards, least, high):
    gain = 1.0
    for position, blocks in shards:
        draws = jax.random.uniform(jax.random.fold_in(jax.random.fold_in(stream_key, 6), position), (blocks,), jnp.float32, least / len(shards), high / len(shards))
        gain = gain * jnp.repeat(jnp.exp(draws), extent[position] // blocks).reshape((-1,) + (1,) * (len(extent) - 1 - position))
    return gain


def centred(key, shape, spread, bound, cuts=(), dtype=jnp.bfloat16):
    array = spread * jax.random.normal(key, shape, jnp.float32)
    if cuts:
        array = array * levels(key, shape, cuts, -0.22, 0.18)
    return jnp.clip(array, -bound, bound).astype(dtype)


def setup_inputs(seed: int = 0) -> dict:
    key_of = jax.random.split(jax.random.key(seed), 7)
    injections = centred(key_of[0], (SCEN, BUSES), 1.0, 6.0, ((1, 32),), jnp.float32)
    transfer_factors = centred(key_of[1], (LINES, BUSES), BUSES ** -0.5, 0.0234375, ((0, 8), (1, 32)), jnp.float32)
    outage_factors = jnp.clip(jax.random.uniform(key_of[2], (LINES, OUTAGES), jnp.float32, -1.0, 1.0) * levels(key_of[2], (LINES, OUTAGES), ((0, 8), (1, 32)), -0.4, 0.0), -1.0, 1.0)
    outage_line = with_ends(jax.random.randint(key_of[3], (OUTAGES,), 0, LINES), jax.random.fold_in(key_of[3], 1), 0, LINES - 1).astype(jnp.int32)
    limit_table = with_ends(jax.random.randint(key_of[4], (TIERS, LINES), 1, 5), jax.random.fold_in(key_of[4], 1), 1, 4).astype(jnp.int32)
    scenario_tier = with_ends(jax.random.randint(key_of[5], (SCEN,), 0, TIERS), jax.random.fold_in(key_of[5], 1), 0, TIERS - 1).astype(jnp.int32)
    return {"injections": injections, "transfer_factors": transfer_factors, "outage_factors": outage_factors, "outage_line": outage_line, "limit_table": limit_table, "scenario_tier": scenario_tier}


def reference(injections, transfer_factors, outage_factors, outage_line, limit_table, scenario_tier):
    flows = jnp.dot(injections, transfer_factors.T, precision=lax.Precision.HIGHEST, preferred_element_type=jnp.float32)
    outage_flows = jnp.take(flows, outage_line, axis=1)
    limits = 0.4 * jnp.take(limit_table, scenario_tier, axis=0).astype(jnp.float32)

    def one_scenario(values):
        flow_row, outage_row, limit_row = values
        post = flow_row[:, None] + outage_factors * outage_row[None, :]
        excess = jnp.maximum(jnp.abs(post) - limit_row[:, None], 0.0)
        weight = 2.0 * excess * jnp.sign(post) / OUTAGES
        return jnp.sum(excess * excess), jnp.sum(weight, axis=1), jnp.sum(weight * outage_factors, axis=0)

    penalty, direct, back = lax.map(one_scenario, (flows, outage_flows, limits))
    mean_penalty = penalty / (LINES * OUTAGES)
    carried = jax.ops.segment_sum(back.T, outage_line, num_segments=LINES).T
    flow_grad = direct + carried
    injection_grad = jnp.dot(flow_grad, transfer_factors, precision=lax.Precision.HIGHEST, preferred_element_type=jnp.float32)
    return injection_grad, mean_penalty
```

```python
import jax
import jax.numpy as jnp
from jax import lax
from jax.experimental import pallas as pl
from jax.experimental.pallas import tpu as pltpu
from jax.sharding import PartitionSpec as P

LINES = 4096
OUTAGES = 8192
SCEN = 64
BUS_COLS = 2176
ROWS = 512
OUTS = 256
CHUNKS = ((0, 640), (640, 512), (1152, 512), (1664, 512))
F32 = jnp.float32
BF16 = jnp.bfloat16
NT = (((1,), (1,)), ((), ()))


def split(value):
    high = value.astype(BF16)
    return high, (value - high.astype(F32)).astype(BF16)


def kernel(
    tier_ref, inj_hbm, tf_hbm, w_hbm, ol_ref, table_ref, grad_ref, pen_ref,
    tf, tf_hi, tf_lo, inj, inj_hl, w, limit, sel,
    part, s1, s2_src, s2, ol_src, ol_all, s3_src, s3,
    flow_t, outage, direct_t, back, pen_acc,
    t1_src, t1, t2_src, t2, t3_src, t3, pen_src, pen1, pen2_src, pen2, back_hl,
    g_src, r1, r2_src, r2,
    load_sem, send_sem, recv_sem, core_send, core_recv, far_send, far_recv,
):
    i = lax.axis_index("line")
    j = lax.axis_index("bus")
    p = j // 2
    zh = lax.rem(j, 2)
    q = zh * 8 + i
    core = lax.rem(i, 2)
    z = i // 2
    half = lax.rem(p, 2)

    def plane_peer(d):
        other = lax.rem(p + d, 16)
        return other, (i, other * 2 + zh)

    def column_peer(d):
        other = lax.rem(q + d, 16)
        return other, (lax.rem(other, 8), p * 2 + other // 8)

    barrier = pltpu.get_barrier_semaphore()

    def greet(d, carry):
        for peer in (plane_peer, column_peer):
            pl.semaphore_signal(
                barrier, inc=1, device_id=peer(d)[1], device_id_type=pl.DeviceIdType.MESH
            )
        return carry

    loads = [pltpu.make_async_copy(inj_hbm, inj, load_sem.at[0])]
    for n in range(2):
        rows = pl.ds(n * 256, 256)
        loads.append(pltpu.make_async_copy(tf_hbm.at[rows], tf.at[rows], load_sem.at[1 + n]))
    loads.append(pltpu.make_async_copy(w_hbm, w, load_sem.at[3]))
    for copy in loads:
        copy.start()
    lax.fori_loop(1, 16, greet, 0)

    def send_all(peer, phase, source, target):
        def one(d, carry):
            other, device = peer(d)
            pltpu.make_async_remote_copy(
                src_ref=source(other),
                dst_ref=target,
                send_sem=send_sem.at[phase],
                recv_sem=recv_sem.at[phase],
                device_id=device,
                device_id_type=pl.DeviceIdType.MESH,
            ).start()
            return carry

        lax.fori_loop(1, 16, one, 0)

    def arrive(phase, buffer):
        view = buffer.at[pl.ds(0, 15)]
        pltpu.make_async_copy(view, view, recv_sem.at[phase]).wait()

    def sent(phase, buffer):
        view = buffer.at[pl.ds(0, 15)]
        pltpu.make_async_copy(view, view, send_sem.at[phase]).wait()

    for tier in range(4):
        for block in range(4):
            row = 0.4 * table_ref[tier : tier + 1, block * 128 : (block + 1) * 128].astype(F32)
            limit[tier, block * 128 : (block + 1) * 128, :] = jnp.broadcast_to(row, (128, 128)).T
    ol_src[...] = ol_ref[...].astype(F32)

    loads[0].wait()
    inj_hi, inj_lo = split(inj[...])
    inj_hl[0:SCEN, :] = inj_hi
    inj_hl[SCEN : 2 * SCEN, :] = inj_lo
    for n in range(2):
        loads[1 + n].wait()

        def cut(step, carry):
            rows = pl.ds(pl.multiple_of(n * 256 + step * 32, 32), 32)
            high, low = split(tf[rows, :])
            tf_hi[rows, :] = high
            tf_lo[rows, :] = low
            return carry

        lax.fori_loop(0, 8, cut, 0)
        rows = slice(n * 256, (n + 1) * 256)
        both = lax.dot_general(inj_hl[...], tf_hi[rows, :], NT, preferred_element_type=F32)
        low = lax.dot_general(inj_hl[0:SCEN, :], tf_lo[rows, :], NT, preferred_element_type=F32)
        flows = both[0:SCEN] + (both[SCEN : 2 * SCEN] + low)
        for group in range(8):
            part[2 * group + n] = flows[group * 8 : (group + 1) * 8]

    pl.semaphore_wait(barrier, 30)
    send_all(plane_peer, 0, lambda other: part.at[other], s1.at[p])
    send_all(plane_peer, 1, lambda other: ol_src, ol_all.at[p])
    s1[p] = part[p]
    ol_all[p] = ol_src[...]
    loads[3].wait()
    direct_t[...] = jnp.zeros_like(direct_t)
    arrive(0, s1)
    s2_src[...] = jnp.sum(s1[...], axis=0)
    send_all(column_peer, 2, lambda other: s2_src, s2.at[q])
    s2[q] = s2_src[...]
    arrive(1, ol_all)

    def pick(block, carry):
        base = (block * 512 + half * 256).astype(F32)
        names = lax.broadcasted_iota(jnp.int32, (256, 256), 0).astype(F32) + base
        for group in range(16):
            hit = names == jnp.broadcast_to(ol_all[group], (256, 256))
            sel[block, :, group * 256 : (group + 1) * 256] = jnp.where(hit, 1.0, 0.0).astype(BF16)
        return carry

    lax.fori_loop(0, 4, pick, 0)
    arrive(2, s2)
    full = [s2[b] + s2[8 + b] for b in range(8)]
    sources = [(b * 4 + k, full[b][:, k * 128 : (k + 1) * 128]) for b in range(8) for k in range(2)]

    def choose(group, carry):
        for k in range(2):
            where = jnp.broadcast_to(ol_all[group, :, k * 128 : (k + 1) * 128], (8, 128)).astype(jnp.int32)
            lane = jnp.bitwise_and(where, 127)
            tile = jnp.right_shift(where, 7) - 2 * half
            out = jnp.zeros((8, 128), F32)
            for name, source in sources:
                out = jnp.where(tile == name, jnp.take_along_axis(source, lane, axis=1), out)
            s3_src[group, 1, :, k * 128 : (k + 1) * 128] = out
        s3_src[group, 0] = s2[i] + s2[8 + i]
        return carry

    lax.fori_loop(0, 16, choose, 0)
    send_all(plane_peer, 3, lambda other: s3_src.at[other], s3.at[p])
    s3[p] = s3_src[p]
    lax.fori_loop(4, 8, pick, 0)
    arrive(3, s3)
    for h in range(2):
        tiles = jnp.concatenate([s3[2 * g + h, 0] for g in range(8)], axis=0)
        flow_t[h * 256 : (h + 1) * 256, 0:SCEN] = tiles.T
    for g in range(8):
        outage[g * 8 : (g + 1) * 8, :] = s3[2 * g, 1] + s3[2 * g + 1, 1]

    lanes = lax.broadcasted_iota(jnp.int32, (8, 128), 1)
    zero = jnp.zeros((8, 128), F32)

    def scenarios(group, carry):
        block = pl.ds(pl.multiple_of(group * 8, 8), 8)
        tile = outage[block, :]
        done = []
        for part_of in range(2):
            first = [part_of * 4 + u for u in range(4)]
            near = [
                [jnp.broadcast_to(tile[u : u + 1, k * 128 : (k + 1) * 128], (8, 128)) for k in range(2)]
                for u in first
            ]
            index = [jnp.full((8, 128), group * 8 + u, jnp.int32) for u in first]
            tiers = [tier_ref[group * 8 + u] for u in first]

            def lines(step, sums):
                sums = list(sums)
                for v in range(4):
                    rows = pl.ds(pl.multiple_of(step * 32 + v * 8, 8), 8)
                    factors = (w[rows, 0:128], w[rows, 128:256])
                    flow = flow_t[rows, :]
                    kept = direct_t[rows, :]
                    for u in range(4):
                        top = limit[tiers[u], rows, :]
                        base = jnp.take_along_axis(flow, index[u], axis=1)
                        over = []
                        for k in range(2):
                            post = base + factors[k] * near[u][k]
                            over.append(post - jnp.minimum(jnp.maximum(post, -top), top))
                            sums[3 * u + k] = sums[3 * u + k] + over[k] * factors[k]
                        sums[3 * u + 2] = sums[3 * u + 2] + (over[0] * over[0] + over[1] * over[1])
                        total = jnp.sum(over[0] + over[1], axis=1, keepdims=True)
                        kept = jnp.where(lanes == index[u], total, kept)
                    direct_t[rows, :] = kept
                return tuple(sums)

            done.extend(lax.fori_loop(0, 16, lines, (zero,) * 12))

        def rows_of(k):
            return jnp.concatenate(
                [jnp.sum(done[3 * u + k], axis=0, keepdims=True) for u in range(8)], axis=0
            )

        back[block, 0:128] = rows_of(0)
        back[block, 128:256] = rows_of(1)
        pen_acc[block, :] = rows_of(2)
        return carry

    lax.fori_loop(0, 8, scenarios, 0)

    for h in range(2):
        turned = direct_t[h * 256 : (h + 1) * 256, :].T
        for g in range(8):
            t1_src[2 * g + h, 0] = turned[g * 8 : (g + 1) * 8, :]
            t1_src[2 * g + h, 1] = back[g * 8 : (g + 1) * 8, :]
    send_all(plane_peer, 4, lambda other: t1_src.at[other], t1.at[p])
    t1[p] = t1_src[p]
    pen_src[:, 0:SCEN] = jnp.sum(pen_acc[...].T, axis=0, keepdims=True)
    pen_src[:, SCEN:128] = jnp.zeros((1, 64), F32)
    send_all(plane_peer, 5, lambda other: pen_src, pen1.at[p])
    pen1[p] = pen_src[...]
    arrive(4, t1)
    for g in range(16):
        high, low = split(t1[g, 1])
        back_hl[:, g * 256 : (g + 1) * 256] = jnp.concatenate([high, low], axis=0)

    def spread(block, carry):
        both = lax.dot_general(back_hl[...], sel[block], NT, preferred_element_type=F32)
        t2_src[block] = both[0:8] + both[8:16]
        return carry

    lax.fori_loop(0, 8, spread, 0)
    t2_src[i] = t2_src[i] + jnp.sum(t1[:, 0], axis=0)
    send_all(column_peer, 6, lambda other: t2_src.at[lax.rem(other, 8)], t2.at[q])
    t2[q] = t2_src[i]
    arrive(5, pen1)
    pen2_src[...] = jnp.sum(pen1[...], axis=0)
    send_all(column_peer, 7, lambda other: pen2_src, pen2.at[q])
    pen2[q] = pen2_src[...]
    arrive(6, t2)
    t3_src[...] = jnp.sum(t2[...], axis=0) * (2.0 / OUTAGES)
    send_all(plane_peer, 8, lambda other: t3_src, t3.at[p])
    t3[p] = t3_src[...]
    arrive(7, pen2)
    pen_ref[...] = jnp.sum(pen2[...], axis=0) * (1.0 / (LINES * OUTAGES))
    arrive(8, t3)

    grad = jnp.concatenate(
        [jnp.concatenate([t3[2 * g + h] for g in range(8)], axis=0) for h in range(2)], axis=1
    )
    grad_hi, grad_lo = split(grad)
    grad_hl = jnp.concatenate([grad_hi, grad_lo], axis=0)
    twin = (i + 1 - 2 * core, j)

    def core_copy(n):
        start, width = CHUNKS[n]
        cols = pl.ds(start, width)
        return pltpu.make_async_remote_copy(
            src_ref=g_src.at[1 - core, :, :, cols],
            dst_ref=r1.at[:, :, cols],
            send_sem=core_send.at[n],
            recv_sem=core_recv.at[n],
            device_id=twin,
            device_id_type=pl.DeviceIdType.MESH,
        )

    def far_copy(n, d):
        start, width = CHUNKS[n]
        cols = pl.ds(start, width)
        other = lax.rem(z + d, 4)
        return pltpu.make_async_remote_copy(
            src_ref=r2_src.at[other, :, cols],
            dst_ref=r2.at[z, :, cols],
            send_sem=far_send.at[n, d - 1],
            recv_sem=far_recv.at[n, d - 1],
            device_id=(other * 2 + core, j),
            device_id_type=pl.DeviceIdType.MESH,
        )

    def pass_on(n):
        start, width = CHUNKS[n]
        cols = slice(start, start + width)
        core_copy(n).wait()
        r2_src[:, :, cols] = g_src[core, :, :, cols] + r1[:, :, cols]
        for d in range(1, 4):
            far_copy(n, d).start()

    for n, (start, width) in enumerate(CHUNKS):
        cols = slice(start, start + width)
        both = jnp.dot(grad_hl, tf_hi[:, cols], preferred_element_type=F32)
        low = jnp.dot(grad_hi, tf_lo[:, cols], preferred_element_type=F32)
        out = both[0:SCEN] + (both[SCEN : 2 * SCEN] + low)
        for a in range(4):
            for c in range(2):
                row = (2 * a + c) * 8
                g_src[c, a, :, cols] = out[row : row + 8]
        core_copy(n).start()
        if n > 0:
            pass_on(n - 1)
    pass_on(len(CHUNKS) - 1)
    r2[z] = r2_src[z]
    for n in range(len(CHUNKS)):
        for d in range(1, 4):
            far_copy(n, d).wait()
    grad_ref[...] = (r2[0] + r2[1]) + (r2[2] + r2[3])
    for phase, buffer in enumerate((s1, ol_all, s2, s3, t1, pen1, t2, pen2, t3)):
        sent(phase, buffer)


def body(injections, transfer_factors, outage_factors, outage_line, limit_table, scenario_tier):
    tile = (8, 256)
    vmem = pltpu.VMEM
    scratch = [
        vmem((ROWS, BUS_COLS), F32),
        vmem((ROWS, BUS_COLS), BF16),
        vmem((ROWS, BUS_COLS), BF16),
        vmem((SCEN, BUS_COLS), F32),
        vmem((2 * SCEN, BUS_COLS), BF16),
        vmem((ROWS, OUTS), F32),
        vmem((4, ROWS, 128), F32),
        vmem((8, 256, 4096), BF16),
        vmem((16,) + tile, F32),
        vmem((16,) + tile, F32),
        vmem(tile, F32),
        vmem((16,) + tile, F32),
        vmem((1, OUTS), F32),
        vmem((16, 1, OUTS), F32),
        vmem((16, 2) + tile, F32),
        vmem((16, 2) + tile, F32),
        vmem((ROWS, 128), F32),
        vmem((SCEN, OUTS), F32),
        vmem((ROWS, 128), F32),
        vmem((SCEN, OUTS), F32),
        vmem((SCEN, 128), F32),
        vmem((16, 2) + tile, F32),
        vmem((16, 2) + tile, F32),
        vmem((8,) + tile, F32),
        vmem((16,) + tile, F32),
        vmem(tile, F32),
        vmem((16,) + tile, F32),
        vmem((1, 128), F32),
        vmem((16, 1, 128), F32),
        vmem((1, 128), F32),
        vmem((16, 1, 128), F32),
        vmem((16, 4096), BF16),
        vmem((2, 4, 8, BUS_COLS), F32),
        vmem((4, 8, BUS_COLS), F32),
        vmem((4, 8, BUS_COLS), F32),
        vmem((4, 8, BUS_COLS), F32),
        pltpu.SemaphoreType.DMA((4,)),
        pltpu.SemaphoreType.DMA((9,)),
        pltpu.SemaphoreType.DMA((9,)),
        pltpu.SemaphoreType.DMA((4,)),
        pltpu.SemaphoreType.DMA((4,)),
        pltpu.SemaphoreType.DMA((4, 3)),
        pltpu.SemaphoreType.DMA((4, 3)),
    ]
    hbm = pl.BlockSpec(memory_space=pl.ANY)
    whole = pl.BlockSpec(memory_space=pltpu.VMEM)
    grad, penalty = pl.pallas_call(
        kernel,
        out_shape=(
            jax.ShapeDtypeStruct((8, BUS_COLS), F32),
            jax.ShapeDtypeStruct((1, 128), F32),
        ),
        in_specs=[pl.BlockSpec(memory_space=pltpu.SMEM), hbm, hbm, hbm, whole, whole],
        out_specs=(whole, whole),
        scratch_shapes=scratch,
        compiler_params=pltpu.CompilerParams(
            collective_id=0, has_side_effects=True, vmem_limit_bytes=60 << 20
        ),
        name="overload",
    )(
        scenario_tier,
        injections,
        transfer_factors,
        outage_factors,
        outage_line.reshape(1, OUTS),
        limit_table,
    )
    return grad, penalty[0, :SCEN]


def solution(mesh):
    return jax.shard_map(
        body,
        mesh=mesh,
        in_specs=(
            P(None, "bus"),
            P("line", "bus"),
            P("line", "bus"),
            P("bus"),
            P(None, "line"),
            P(),
        ),
        out_specs=(P("line", "bus"), P()),
        check_vma=False,
    )
```

```python
import jax
import jax.numpy as jnp
from jax import lax
from jax.experimental import pallas as pl
from jax.experimental.pallas import tpu as pltpu
from jax.sharding import PartitionSpec as P

LINES = 4096
OUTAGES = 8192
SCEN = 64
BUS_COLS = 2176
ROWS = 512
OUTS = 256
CHUNKS = ((0, 640), (640, 512), (1152, 512), (1664, 512))
F32 = jnp.float32
BF16 = jnp.bfloat16
NT = (((1,), (1,)), ((), ()))


def split(value):
    high = value.astype(BF16)
    return high, (value - high.astype(F32)).astype(BF16)


def kernel(
    tier_ref, inj_hbm, tf_hbm, w_hbm, ol_ref, table_ref, grad_ref, pen_ref,
    tf, tf_hi, tf_lo, inj, inj_hl, w, w_t, w_parts, w_wide, limit_t, lane_hit, spread_in,
    part, s1, s2_src, s2, ol_src, ol_all, s3_src, s3,
    flow_t, outage_t, direct_t, back_rows, back_t,
    t1_src, t1, t2_src, t2, t3_src, t3, pen_src, pen1, pen2_src, pen2,
    g_src, r1, r2_src, r2,
    load_sem, send_sem, recv_sem, core_send, core_recv, far_send, far_recv,
):
    i = lax.axis_index("line")
    j = lax.axis_index("bus")
    p = j // 2
    zh = lax.rem(j, 2)
    q = zh * 8 + i
    core = lax.rem(i, 2)
    z = i // 2
    half = lax.rem(p, 2)

    def plane_peer(d):
        other = lax.rem(p + d, 16)
        return other, (i, other * 2 + zh)

    def column_peer(d):
        other = lax.rem(q + d, 16)
        return other, (lax.rem(other, 8), p * 2 + other // 8)

    barrier = pltpu.get_barrier_semaphore()

    def greet(d, carry):
        for peer in (plane_peer, column_peer):
            pl.semaphore_signal(
                barrier, inc=1, device_id=peer(d)[1], device_id_type=pl.DeviceIdType.MESH
            )
        return carry

    loads = [pltpu.make_async_copy(inj_hbm, inj, load_sem.at[0])]
    for n in range(2):
        rows = pl.ds(n * 256, 256)
        loads.append(pltpu.make_async_copy(tf_hbm.at[rows], tf.at[rows], load_sem.at[1 + n]))
    loads.append(pltpu.make_async_copy(w_hbm, w, load_sem.at[3]))
    for copy in loads:
        copy.start()
    lax.fori_loop(1, 16, greet, 0)

    def send_all(peer, phase, source, target):
        def one(d, carry):
            other, device = peer(d)
            pltpu.make_async_remote_copy(
                src_ref=source(other),
                dst_ref=target,
                send_sem=send_sem.at[phase],
                recv_sem=recv_sem.at[phase],
                device_id=device,
                device_id_type=pl.DeviceIdType.MESH,
            ).start()
            return carry

        lax.fori_loop(1, 16, one, 0)

    def arrive(phase, buffer):
        view = buffer.at[pl.ds(0, 15)]
        pltpu.make_async_copy(view, view, recv_sem.at[phase]).wait()

    def sent(phase, buffer):
        view = buffer.at[pl.ds(0, 15)]
        pltpu.make_async_copy(view, view, send_sem.at[phase]).wait()

    tiers = jnp.concatenate([tier_ref[...], tier_ref[...]], axis=1)
    left = lax.broadcasted_iota(jnp.int32, (128, 128), 1) < SCEN
    for block in range(2):
        rows = slice(block * 128, (block + 1) * 128)
        value = jnp.zeros((128, 128), F32)
        for tier in range(4):
            pair = [
                jnp.broadcast_to(
                    0.4 * table_ref[tier : tier + 1, h * 256 + block * 128 : h * 256 + block * 128 + 128].astype(F32),
                    (128, 128),
                ).T
                for h in range(2)
            ]
            value = jnp.where(tiers == tier, jnp.where(left, pair[0], pair[1]), value)
        limit_t[rows, :] = value
    ol_src[...] = ol_ref[...].astype(F32)

    loads[0].wait()
    inj_hi, inj_lo = split(inj[...])
    inj_hl[0:SCEN, :] = inj_hi
    inj_hl[SCEN : 2 * SCEN, :] = inj_lo
    for n in range(2):
        loads[1 + n].wait()

        def cut(step, carry):
            rows = pl.ds(pl.multiple_of(n * 256 + step * 32, 32), 32)
            high, low = split(tf[rows, :])
            tf_hi[rows, :] = high
            tf_lo[rows, :] = low
            return carry

        lax.fori_loop(0, 8, cut, 0)
        rows = slice(n * 256, (n + 1) * 256)
        both = lax.dot_general(inj_hl[...], tf_hi[rows, :], NT, preferred_element_type=F32)
        low = lax.dot_general(inj_hl[0:SCEN, :], tf_lo[rows, :], NT, preferred_element_type=F32)
        flows = both[0:SCEN] + (both[SCEN : 2 * SCEN] + low)
        for group in range(8):
            part[2 * group + n] = flows[group * 8 : (group + 1) * 8]

    key_row = lax.broadcasted_iota(jnp.int32, (256, 256), 0)
    key_col = lax.broadcasted_iota(jnp.int32, (256, 256), 1)
    same_half = jnp.bitwise_and(jnp.right_shift(key_row, 5) - jnp.right_shift(key_col, 6), 1) == 0
    key = jnp.where(same_half, jnp.bitwise_and(key_row, 31) - jnp.right_shift(key_col, 7), -1)

    def widen_start():
        w_t[...] = w[...].T

        def group(g, carry):
            piece = w_t[pl.ds(pl.multiple_of(g * 32, 32), 32), :]
            high = piece.astype(BF16).astype(F32)
            rest = piece - high
            middle = rest.astype(BF16).astype(F32)
            stack = [
                value[:, h * 256 : (h + 1) * 256]
                for value in (high, middle, rest - middle)
                for h in range(2)
            ]
            stack.append(jnp.zeros((64, 256), F32))
            w_parts[g] = jnp.concatenate(stack, axis=0).T.astype(BF16)
            return carry

        lax.fori_loop(0, 8, group, 0)

    def widen(step, carry):
        ones = jnp.where(key == 2 * step, 1.0, 0.0).astype(BF16)
        for g in range(8):
            wide = jnp.dot(w_parts[g], ones, preferred_element_type=F32)
            w_wide[g * 32 + 2 * step] = wide[:, 0:128]
            w_wide[g * 32 + 2 * step + 1] = wide[:, 128:256]
        return carry

    pl.semaphore_wait(barrier, 30)
    send_all(plane_peer, 0, lambda other: part.at[other], s1.at[p])
    send_all(plane_peer, 1, lambda other: ol_src, ol_all.at[p])
    s1[p] = part[p]
    ol_all[p] = ol_src[...]
    loads[3].wait()
    widen_start()
    lax.fori_loop(0, 4, widen, 0)
    arrive(0, s1)
    s2_src[...] = jnp.sum(s1[...], axis=0)
    send_all(column_peer, 2, lambda other: s2_src, s2.at[q])
    s2[q] = s2_src[...]
    arrive(1, ol_all)

    lax.fori_loop(4, 10, widen, 0)
    arrive(2, s2)
    full = [s2[b] + s2[8 + b] for b in range(8)]
    sources = [(b * 4 + k, full[b][:, k * 128 : (k + 1) * 128]) for b in range(8) for k in range(2)]

    def choose(group, carry):
        for k in range(2):
            where = jnp.broadcast_to(ol_all[group, :, k * 128 : (k + 1) * 128], (8, 128)).astype(jnp.int32)
            lane = jnp.bitwise_and(where, 127)
            tile = jnp.right_shift(where, 7) - 2 * half
            out = jnp.zeros((8, 128), F32)
            for name, source in sources:
                out = jnp.where(tile == name, jnp.take_along_axis(source, lane, axis=1), out)
            s3_src[group, 1, :, k * 128 : (k + 1) * 128] = out
        s3_src[group, 0] = s2[i] + s2[8 + i]
        return carry

    lax.fori_loop(0, 16, choose, 0)
    send_all(plane_peer, 3, lambda other: s3_src.at[other], s3.at[p])
    s3[p] = s3_src[p]
    lax.fori_loop(10, 16, widen, 0)
    arrive(3, s3)
    tiles = jnp.concatenate([s3[2 * g + h, 0] for h in range(2) for g in range(8)], axis=0)
    flow_t[...] = tiles.T
    picked = jnp.concatenate([s3[2 * g, 1] + s3[2 * g + 1, 1] for g in range(8)], axis=0)
    outage_t[...] = jnp.concatenate([picked, picked], axis=0).T

    penalty = jnp.zeros((8, 128), F32)
    for block in range(4):
        slabs = [slice(block * 64 + v * 8, block * 64 + v * 8 + 8) for v in range(8)]
        flow = [flow_t[rows, :] for rows in slabs]
        top = [limit_t[rows, :] for rows in slabs]
        low = [-value for value in top]

        def outages(step, carry):
            direct = list(carry[:8])
            squares = carry[8]
            eight = pl.ds(pl.multiple_of(step * 8, 8), 8)
            near = outage_t[eight, :]
            sums = []
            for u in range(8):
                name = step * 8 + u
                here = jnp.broadcast_to(near[u : u + 1, :], (8, 128))
                back = None
                for v in range(8):
                    factor = w_wide[name, slabs[v], :]
                    post = factor * here + flow[v]
                    over = post - jnp.minimum(jnp.maximum(post, low[v]), top[v])
                    direct[v] = direct[v] + over
                    term = over * factor
                    back = term if back is None else back + term
                    squares = squares + over * over
                if block > 0:
                    back = back + back_rows[name]
                if block < 3:
                    back_rows[name] = back
                else:
                    sums.append(jnp.sum(back, axis=0, keepdims=True))
            if block == 3:
                back_t[eight, :] = jnp.concatenate(sums, axis=0)
            return tuple(direct) + (squares,)

        start = tuple(jnp.zeros((8, 128), F32) for _ in range(8)) + (penalty,)
        result = lax.fori_loop(0, 32, outages, start)
        for v in range(8):
            direct_t[slabs[v], :] = result[v]
        penalty = result[8]

    direct = direct_t[...].T
    back = back_t[...].T
    back = back[0:SCEN] + back[SCEN : 2 * SCEN]
    for h in range(2):
        for g in range(8):
            t1_src[2 * g + h, 0] = direct[h * SCEN + g * 8 : h * SCEN + g * 8 + 8, :]
            t1_src[2 * g + h, 1] = back[g * 8 : (g + 1) * 8, :]
    send_all(plane_peer, 4, lambda other: t1_src.at[other], t1.at[p])
    t1[p] = t1_src[p]
    pen_src[...] = jnp.sum(penalty, axis=0, keepdims=True)
    send_all(plane_peer, 5, lambda other: pen_src, pen1.at[p])
    pen1[p] = pen_src[...]
    def mark(group, carry):
        lane = jnp.bitwise_and(jnp.broadcast_to(ol_all[group], (128, 256)).astype(jnp.int32), 127)
        hit = lane == lax.broadcasted_iota(jnp.int32, (128, 256), 0)
        lane_hit[group] = jnp.where(hit, 1.0, 0.0).astype(BF16)
        return carry

    lax.fori_loop(0, 16, mark, 0)
    arrive(4, t1)

    def sort(group, carry):
        high, low = split(t1[group, 1])
        both = jnp.concatenate([high.astype(F32), low.astype(F32)], axis=0)
        tile = jnp.right_shift(jnp.broadcast_to(ol_all[group], (16, 256)).astype(jnp.int32), 7) - 2 * half
        for t in range(16):
            name = (t // 2) * 4 + t % 2
            spread_in[group, t * 16 : (t + 1) * 16, :] = jnp.where(tile == name, both, 0.0).astype(BF16)
        return carry

    lax.fori_loop(0, 16, sort, 0)
    total = jnp.zeros((256, 128), F32)
    for group in range(16):
        total = total + lax.dot_general(
            spread_in[group], lane_hit[group], NT, preferred_element_type=F32
        )
    for t in range(16):
        cols = slice((t % 2) * 128, (t % 2) * 128 + 128)
        t2_src[t // 2, :, cols] = total[t * 16 : t * 16 + 8] + total[t * 16 + 8 : t * 16 + 16]
    t2_src[i] = t2_src[i] + jnp.sum(t1[:, 0], axis=0)
    send_all(column_peer, 6, lambda other: t2_src.at[lax.rem(other, 8)], t2.at[q])
    t2[q] = t2_src[i]
    arrive(5, pen1)
    pen2_src[...] = jnp.sum(pen1[...], axis=0)
    send_all(column_peer, 7, lambda other: pen2_src, pen2.at[q])
    pen2[q] = pen2_src[...]
    arrive(6, t2)
    t3_src[...] = jnp.sum(t2[...], axis=0) * (2.0 / OUTAGES)
    send_all(plane_peer, 8, lambda other: t3_src, t3.at[p])
    t3[p] = t3_src[...]
    arrive(7, pen2)
    both = jnp.sum(pen2[...], axis=0) * (1.0 / (LINES * OUTAGES))
    pen_ref[...] = both[:, 0:SCEN] + both[:, SCEN:128]
    arrive(8, t3)

    grad = jnp.concatenate(
        [jnp.concatenate([t3[2 * g + h] for g in range(8)], axis=0) for h in range(2)], axis=1
    )
    grad_hi, grad_lo = split(grad)
    grad_hl = jnp.concatenate([grad_hi, grad_lo], axis=0)
    twin = (i + 1 - 2 * core, j)

    def core_copy(n):
        start, width = CHUNKS[n]
        cols = pl.ds(start, width)
        return pltpu.make_async_remote_copy(
            src_ref=g_src.at[1 - core, :, :, cols],
            dst_ref=r1.at[:, :, cols],
            send_sem=core_send.at[n],
            recv_sem=core_recv.at[n],
            device_id=twin,
            device_id_type=pl.DeviceIdType.MESH,
        )

    def far_copy(n, d):
        start, width = CHUNKS[n]
        cols = pl.ds(start, width)
        other = lax.rem(z + d, 4)
        return pltpu.make_async_remote_copy(
            src_ref=r2_src.at[other, :, cols],
            dst_ref=r2.at[z, :, cols],
            send_sem=far_send.at[n, d - 1],
            recv_sem=far_recv.at[n, d - 1],
            device_id=(other * 2 + core, j),
            device_id_type=pl.DeviceIdType.MESH,
        )

    def pass_on(n):
        start, width = CHUNKS[n]
        cols = slice(start, start + width)
        core_copy(n).wait()
        r2_src[:, :, cols] = g_src[core, :, :, cols] + r1[:, :, cols]
        for d in range(1, 4):
            far_copy(n, d).start()

    for n, (start, width) in enumerate(CHUNKS):
        cols = slice(start, start + width)
        both = jnp.dot(grad_hl, tf_hi[:, cols], preferred_element_type=F32)
        low = jnp.dot(grad_hi, tf_lo[:, cols], preferred_element_type=F32)
        out = both[0:SCEN] + (both[SCEN : 2 * SCEN] + low)
        for a in range(4):
            for c in range(2):
                row = (2 * a + c) * 8
                g_src[c, a, :, cols] = out[row : row + 8]
        core_copy(n).start()
        if n > 0:
            pass_on(n - 1)
    pass_on(len(CHUNKS) - 1)
    r2[z] = r2_src[z]
    for n in range(len(CHUNKS)):
        for d in range(1, 4):
            far_copy(n, d).wait()
    grad_ref[...] = (r2[0] + r2[1]) + (r2[2] + r2[3])
    for phase, buffer in enumerate((s1, ol_all, s2, s3, t1, pen1, t2, pen2, t3)):
        sent(phase, buffer)


def body(injections, transfer_factors, outage_factors, outage_line, limit_table, scenario_tier):
    tile = (8, 256)
    vmem = pltpu.VMEM
    scratch = [
        vmem((ROWS, BUS_COLS), F32),
        vmem((ROWS, BUS_COLS), BF16),
        vmem((ROWS, BUS_COLS), BF16),
        vmem((SCEN, BUS_COLS), F32),
        vmem((2 * SCEN, BUS_COLS), BF16),
        vmem((ROWS, OUTS), F32),
        vmem((OUTS, ROWS), F32),
        vmem((8, 256, 256), BF16),
        vmem((OUTS, 256, 128), F32),
        vmem((256, 128), F32),
        vmem((16, 128, 256), BF16),
        vmem((16, 256, 256), BF16),
        vmem((16,) + tile, F32),
        vmem((16,) + tile, F32),
        vmem(tile, F32),
        vmem((16,) + tile, F32),
        vmem((1, OUTS), F32),
        vmem((16, 1, OUTS), F32),
        vmem((16, 2) + tile, F32),
        vmem((16, 2) + tile, F32),
        vmem((256, 128), F32),
        vmem((OUTS, 128), F32),
        vmem((256, 128), F32),
        vmem((OUTS, 8, 128), F32),
        vmem((OUTS, 128), F32),
        vmem((16, 2) + tile, F32),
        vmem((16, 2) + tile, F32),
        vmem((8,) + tile, F32),
        vmem((16,) + tile, F32),
        vmem(tile, F32),
        vmem((16,) + tile, F32),
        vmem((1, 128), F32),
        vmem((16, 1, 128), F32),
        vmem((1, 128), F32),
        vmem((16, 1, 128), F32),
        vmem((2, 4, 8, BUS_COLS), F32),
        vmem((4, 8, BUS_COLS), F32),
        vmem((4, 8, BUS_COLS), F32),
        vmem((4, 8, BUS_COLS), F32),
        pltpu.SemaphoreType.DMA((4,)),
        pltpu.SemaphoreType.DMA((9,)),
        pltpu.SemaphoreType.DMA((9,)),
        pltpu.SemaphoreType.DMA((4,)),
        pltpu.SemaphoreType.DMA((4,)),
        pltpu.SemaphoreType.DMA((4, 3)),
        pltpu.SemaphoreType.DMA((4, 3)),
    ]
    hbm = pl.BlockSpec(memory_space=pl.ANY)
    whole = pl.BlockSpec(memory_space=pltpu.VMEM)
    grad, penalty = pl.pallas_call(
        kernel,
        out_shape=(
            jax.ShapeDtypeStruct((8, BUS_COLS), F32),
            jax.ShapeDtypeStruct((1, SCEN), F32),
        ),
        in_specs=[whole, hbm, hbm, hbm, whole, whole],
        out_specs=(whole, whole),
        scratch_shapes=scratch,
        compiler_params=pltpu.CompilerParams(
            collective_id=0, has_side_effects=True, vmem_limit_bytes=60 << 20
        ),
        name="overload",
    )(
        scenario_tier.reshape(1, SCEN),
        injections,
        transfer_factors,
        outage_factors,
        outage_line.reshape(1, OUTS),
        limit_table,
    )
    return grad, penalty.reshape(SCEN)


def solution(mesh):
    return jax.shard_map(
        body,
        mesh=mesh,
        in_specs=(
            P(None, "bus"),
            P("line", "bus"),
            P("line", "bus"),
            P("bus"),
            P(None, "line"),
            P(),
        ),
        out_specs=(P("line", "bus"), P()),
        check_vma=False,
    )
```

```python
import jax
import jax.numpy as jnp
from jax import lax
from jax.experimental import pallas as pl
from jax.experimental.pallas import tpu as pltpu
from jax.sharding import PartitionSpec as P

LINES = 4096
OUTAGES = 8192
SCEN = 64
BUS_COLS = 2176
ROWS = 512
OUTS = 256
CHUNKS = ((0, 256), (256, 384), (640, 512), (1152, 512), (1664, 512))
F32 = jnp.float32
BF16 = jnp.bfloat16
NT = (((1,), (1,)), ((), ()))


def torus(size, step):
    return min(step, size - step)


PLANE = sorted(
    [(dy, dx) for dy in range(4) for dx in range(4) if dy + dx],
    key=lambda step: -torus(4, step[0]) - torus(4, step[1]),
)
COLUMN = sorted(
    [(dz, dc) for dz in range(8) for dc in range(2) if dz + dc], key=lambda step: -torus(8, step[0])
)


def split(value):
    high = value.astype(BF16)
    return high, (value - high.astype(F32)).astype(BF16)


def kernel(
    tier_hbm, inj_hbm, tf_hbm, w_hbm, ol_hbm, table_hbm, grad_ref, pen_ref,
    tier_ref, ol_ref, table_ref,
    tf, tf_hi, tf_lo, inj, inj_hl, w, w_t, w_parts, w_wide, limit_t, lane_hit, spread_in,
    part, s1, s2_src, s2, ol_src, ol_all, s3_src, s3, flow_src, flow_in, lane_of, tile_of,
    flow_t, outage_t, direct_t, back_rows, back_t,
    t1_src, t1, direct_src, direct_in, t2_src, t2, t3_src, t3, pen_src, pen1, pen2_src, pen2,
    g_src, r1, r2_src, r2,
    load_sem, send_sem, recv_sem, near_recv, far_back, core_send, core_recv, far_send, far_recv,
):
    i = lax.axis_index("line")
    j = lax.axis_index("bus")
    p = j // 2
    zh = lax.rem(j, 2)
    q = zh * 8 + i
    core = lax.rem(i, 2)
    z = i // 2
    half = lax.rem(p, 2)

    def plane_peer(step):
        other = lax.rem(p // 4 + step[0], 4) * 4 + lax.rem(p + step[1], 4)
        return other, (i, other * 2 + zh)

    def column_peer(step):
        chip = lax.rem(zh * 4 + z + step[0], 8)
        line = lax.rem(chip, 4) * 2 + lax.rem(core + step[1], 2)
        return (chip // 4) * 8 + line, (line, p * 2 + chip // 4)

    barrier = pltpu.get_barrier_semaphore()

    for peer, steps in ((plane_peer, PLANE), (column_peer, COLUMN)):
        for step in steps:
            pl.semaphore_signal(
                barrier, inc=1, device_id=peer(step)[1], device_id_type=pl.DeviceIdType.MESH
            )
    pairs = [(inj_hbm, inj)]
    pairs += [(tf_hbm.at[pl.ds(n * 128, 128)], tf.at[pl.ds(n * 128, 128)]) for n in range(4)]
    pairs += [(ol_hbm, ol_ref), (w_hbm, w), (table_hbm, table_ref), (tier_hbm, tier_ref)]
    loads = [pltpu.make_async_copy(a, b, load_sem.at[n]) for n, (a, b) in enumerate(pairs)]
    for copy in loads:
        copy.start()

    def send_all(peer, phase, source, target, arrived=None):
        for step in PLANE if peer is plane_peer else COLUMN:
            other, device = peer(step)
            pltpu.make_async_remote_copy(
                src_ref=source(other),
                dst_ref=target,
                send_sem=send_sem.at[phase],
                recv_sem=recv_sem.at[phase] if arrived is None else arrived,
                device_id=device,
                device_id_type=pl.DeviceIdType.MESH,
            ).start()

    def arrive_one(semaphore, view):
        pltpu.make_async_copy(view, view, semaphore).wait()

    def arrive(phase, buffer):
        view = buffer.at[pl.ds(0, 15)]
        pltpu.make_async_copy(view, view, recv_sem.at[phase]).wait()

    def sent(phase, buffer):
        view = buffer.at[pl.ds(0, 15)]
        pltpu.make_async_copy(view, view, send_sem.at[phase]).wait()


    loads[0].wait()
    inj_hi, inj_lo = split(inj[...])
    inj_hl[0:SCEN, :] = inj_hi
    inj_hl[SCEN : 2 * SCEN, :] = inj_lo
    for n in range(2):

        def cut(step, carry):
            rows = pl.ds(pl.multiple_of(step * 32, 32), 32)
            high, low = split(tf[rows, :])
            tf_hi[rows, :] = high
            tf_lo[rows, :] = low
            return carry

        for m in (2 * n, 2 * n + 1):
            loads[1 + m].wait()
            lax.fori_loop(4 * m, 4 * m + 4, cut, 0)
        rows = slice(n * 256, (n + 1) * 256)
        both = lax.dot_general(inj_hl[...], tf_hi[rows, :], NT, preferred_element_type=F32)
        low = lax.dot_general(inj_hl[0:SCEN, :], tf_lo[rows, :], NT, preferred_element_type=F32)
        flows = both[0:SCEN] + (both[SCEN : 2 * SCEN] + low)
        for group in range(8):
            part[2 * group + n] = flows[group * 8 : (group + 1) * 8]

    key_row = lax.broadcasted_iota(jnp.int32, (256, 256), 0)
    key_col = lax.broadcasted_iota(jnp.int32, (256, 256), 1)
    same_half = jnp.bitwise_and(jnp.right_shift(key_row, 5) - jnp.right_shift(key_col, 6), 1) == 0
    key = jnp.where(same_half, jnp.bitwise_and(key_row, 31) - jnp.right_shift(key_col, 7), -1)

    def widen_start():
        w_t[...] = w[...].T

        def group(g, carry):
            piece = w_t[pl.ds(pl.multiple_of(g * 32, 32), 32), :]
            high = piece.astype(BF16).astype(F32)
            rest = piece - high
            middle = rest.astype(BF16).astype(F32)
            stack = [
                value[:, h * 256 : (h + 1) * 256]
                for value in (high, middle, rest - middle)
                for h in range(2)
            ]
            stack.append(jnp.zeros((64, 256), F32))
            w_parts[g] = jnp.concatenate(stack, axis=0).T.astype(BF16)
            return carry

        lax.fori_loop(0, 8, group, 0)

    def widen(step, carry):
        ones = jnp.where(key == 2 * step, 1.0, 0.0).astype(BF16)
        for g in range(8):
            wide = jnp.dot(w_parts[g], ones, preferred_element_type=F32)
            w_wide[g * 32 + 2 * step] = wide[:, 0:128]
            w_wide[g * 32 + 2 * step + 1] = wide[:, 128:256]
        return carry

    pl.semaphore_wait(barrier, 30)
    send_all(plane_peer, 0, lambda other: part.at[other], s1.at[p])
    loads[5].wait()
    ol_src[...] = ol_ref[...].astype(F32)
    send_all(plane_peer, 1, lambda other: ol_src, ol_all.at[p])
    s1[p] = part[p]
    ol_all[p] = ol_src[...]
    for copy in loads[6:]:
        copy.wait()
    tiers = jnp.concatenate([tier_ref[...], tier_ref[...]], axis=1)
    left = lax.broadcasted_iota(jnp.int32, (128, 128), 1) < SCEN
    for block in range(2):
        rows = slice(block * 128, (block + 1) * 128)
        value = jnp.zeros((128, 128), F32)
        for tier in range(4):
            pair = [
                jnp.broadcast_to(
                    0.4 * table_ref[tier : tier + 1, h * 256 + block * 128 : h * 256 + block * 128 + 128].astype(F32),
                    (128, 128),
                ).T
                for h in range(2)
            ]
            value = jnp.where(tiers == tier, jnp.where(left, pair[0], pair[1]), value)
        limit_t[rows, :] = value
    widen_start()
    lax.fori_loop(0, 2, widen, 0)
    arrive(0, s1)
    s2_src[...] = jnp.sum(s1[...], axis=0)
    send_all(column_peer, 2, lambda other: s2_src, s2.at[q], near_recv.at[q])
    s2[q] = s2_src[...]
    arrive(1, ol_all)

    lax.fori_loop(2, 7, widen, 0)
    def names(group, carry):
        where = jnp.broadcast_to(ol_all[group], (8, 256)).astype(jnp.int32)
        lane_of[group] = jnp.bitwise_and(where, 127)
        tile_of[group] = jnp.right_shift(where, 7)
        return carry

    lax.fori_loop(0, 16, names, 0)
    for ahead in (2, 1, 3, 0):
        blocks = [lax.rem(z + ahead, 4) * 2 + c for c in range(2)]
        sources = []
        for block in blocks:
            for h in range(2):
                slot = h * 8 + block

                @pl.when(slot != q)
                def _():
                    arrive_one(near_recv.at[slot], s2.at[slot])

            full = s2[block] + s2[8 + block]
            for k in range(2):
                sources.append((block * 4 + 2 * half + k, full[:, k * 128 : (k + 1) * 128]))
        for group in range(16):
            for k in range(2):
                cols = slice(k * 128, (k + 1) * 128)
                lane = lane_of[group, :, cols]
                tile = tile_of[group, :, cols]
                out = jnp.zeros((8, 128), F32) if ahead == 2 else s3_src[group, :, cols]
                for name, source in sources:
                    out = jnp.where(tile == name, jnp.take_along_axis(source, lane, axis=1), out)
                s3_src[group, :, cols] = out
    flow_src[...] = s2[i] + s2[8 + i]
    send_all(plane_peer, 3, lambda other: s3_src.at[other], s3.at[p])
    send_all(plane_peer, 9, lambda other: flow_src, flow_in.at[p])
    s3[p] = s3_src[p]
    flow_in[p] = flow_src[...]
    lax.fori_loop(7, 16, widen, 0)
    arrive(3, s3)
    arrive(9, flow_in)
    tiles = jnp.concatenate([flow_in[2 * g + h] for h in range(2) for g in range(8)], axis=0)
    flow_t[...] = tiles.T
    picked = jnp.concatenate([s3[2 * g] + s3[2 * g + 1] for g in range(8)], axis=0)
    outage_t[...] = jnp.concatenate([picked, picked], axis=0).T

    penalty = jnp.zeros((8, 128), F32)
    for block in range(4):
        slabs = [slice(block * 64 + v * 8, block * 64 + v * 8 + 8) for v in range(8)]
        flow = [flow_t[rows, :] for rows in slabs]
        top = [limit_t[rows, :] for rows in slabs]
        low = [-value for value in top]

        def outages(step, carry):
            direct = list(carry[:8])
            squares = carry[8]
            eight = pl.ds(pl.multiple_of(step * 8, 8), 8)
            near = outage_t[eight, :]
            sums = []
            for u in range(8):
                name = step * 8 + u
                here = jnp.broadcast_to(near[u : u + 1, :], (8, 128))
                back = None
                for v in range(8):
                    factor = w_wide[name, slabs[v], :]
                    post = factor * here + flow[v]
                    over = post - jnp.minimum(jnp.maximum(post, low[v]), top[v])
                    direct[v] = direct[v] + over
                    term = over * factor
                    back = term if back is None else back + term
                    squares = squares + over * over
                if block > 0:
                    back = back + back_rows[name]
                if block < 3:
                    back_rows[name] = back
                else:
                    sums.append(jnp.sum(back, axis=0, keepdims=True))
            if block == 3:
                back_t[eight, :] = jnp.concatenate(sums, axis=0)
            return tuple(direct) + (squares,)

        start = tuple(jnp.zeros((8, 128), F32) for _ in range(8)) + (penalty,)
        result = lax.fori_loop(0, 32, outages, start)
        for v in range(8):
            direct_t[slabs[v], :] = result[v]
        penalty = result[8]

    back = back_t[...].T
    back = back[0:SCEN] + back[SCEN : 2 * SCEN]
    for g in range(8):
        t1_src[g] = back[g * 8 : (g + 1) * 8, :]
    send_all(plane_peer, 4, lambda other: t1_src.at[other // 2], t1.at[p], far_back.at[p])
    t1[p] = t1_src[p // 2]
    direct = direct_t[...].T
    for h in range(2):
        for g in range(8):
            direct_src[2 * g + h] = direct[h * SCEN + g * 8 : h * SCEN + g * 8 + 8, :]
    send_all(plane_peer, 10, lambda other: direct_src.at[other], direct_in.at[p])
    direct_in[p] = direct_src[p]
    pen_src[...] = jnp.sum(penalty, axis=0, keepdims=True)
    send_all(plane_peer, 5, lambda other: pen_src, pen1.at[p])
    pen1[p] = pen_src[...]
    def mark(group, carry):
        lane = jnp.bitwise_and(jnp.broadcast_to(ol_all[group], (128, 256)).astype(jnp.int32), 127)
        hit = lane == lax.broadcasted_iota(jnp.int32, (128, 256), 0)
        lane_hit[group] = jnp.where(hit, 1.0, 0.0).astype(BF16)
        return carry

    lax.fori_loop(0, 16, mark, 0)

    total = jnp.zeros((256, 128), F32)
    for step in [(0, 0)] + PLANE[::-1]:
        group = plane_peer(step)[0]
        if step != (0, 0):
            arrive_one(far_back.at[group], t1.at[group])
        high, low = split(t1[group])
        both = jnp.concatenate([high.astype(F32), low.astype(F32)], axis=0)
        tile = jnp.concatenate([tile_of[group], tile_of[group]], axis=0) - 2 * half
        for t in range(16):
            name = (t // 2) * 4 + t % 2
            spread_in[group, t * 16 : (t + 1) * 16, :] = jnp.where(tile == name, both, 0.0).astype(BF16)
        total = total + lax.dot_general(
            spread_in[group], lane_hit[group], NT, preferred_element_type=F32
        )
    for t in range(16):
        cols = slice((t % 2) * 128, (t % 2) * 128 + 128)
        t2_src[t // 2, :, cols] = total[t * 16 : t * 16 + 8] + total[t * 16 + 8 : t * 16 + 16]
    arrive(10, direct_in)
    t2_src[i] = t2_src[i] + jnp.sum(direct_in[...], axis=0)
    send_all(column_peer, 6, lambda other: t2_src.at[lax.rem(other, 8)], t2.at[q])
    t2[q] = t2_src[i]
    arrive(5, pen1)
    pen2_src[...] = jnp.sum(pen1[...], axis=0)
    send_all(column_peer, 7, lambda other: pen2_src, pen2.at[q])
    pen2[q] = pen2_src[...]
    arrive(6, t2)
    t3_src[...] = jnp.sum(t2[...], axis=0) * (2.0 / OUTAGES)
    send_all(plane_peer, 8, lambda other: t3_src, t3.at[p])
    t3[p] = t3_src[...]
    arrive(7, pen2)
    both = jnp.sum(pen2[...], axis=0) * (1.0 / (LINES * OUTAGES))
    pen_ref[...] = both[:, 0:SCEN] + both[:, SCEN:128]
    arrive(8, t3)

    grad = jnp.concatenate(
        [jnp.concatenate([t3[2 * g + h] for g in range(8)], axis=0) for h in range(2)], axis=1
    )
    grad_hi, grad_lo = split(grad)
    grad_hl = jnp.concatenate([grad_hi, grad_lo], axis=0)
    twin = (i + 1 - 2 * core, j)

    def core_copy(n):
        start, width = CHUNKS[n]
        cols = pl.ds(start, width)
        return pltpu.make_async_remote_copy(
            src_ref=g_src.at[1 - core, :, :, cols],
            dst_ref=r1.at[:, :, cols],
            send_sem=core_send.at[n],
            recv_sem=core_recv.at[n],
            device_id=twin,
            device_id_type=pl.DeviceIdType.MESH,
        )

    right = z // 2
    others = (3 - 3 * right, 2 - right, z + 1 - 2 * lax.rem(z, 2))

    def far_copy(n, d):
        start, width = CHUNKS[n]
        cols = pl.ds(start, width)
        return pltpu.make_async_remote_copy(
            src_ref=r2_src.at[others[d], :, cols],
            dst_ref=r2.at[z, :, cols],
            send_sem=far_send.at[n, d],
            recv_sem=far_recv.at[n, z],
            device_id=(others[d] * 2 + core, j),
            device_id_type=pl.DeviceIdType.MESH,
        )

    def pass_on(n):
        start, width = CHUNKS[n]
        cols = slice(start, start + width)
        core_copy(n).wait()
        r2_src[:, :, cols] = g_src[core, :, :, cols] + r1[:, :, cols]
        for d in range(3):
            far_copy(n, d).start()

    for n, (start, width) in enumerate(CHUNKS):
        cols = slice(start, start + width)
        both = jnp.dot(grad_hl, tf_hi[:, cols], preferred_element_type=F32)
        low = jnp.dot(grad_hi, tf_lo[:, cols], preferred_element_type=F32)
        out = both[0:SCEN] + (both[SCEN : 2 * SCEN] + low)
        for a in range(4):
            for c in range(2):
                row = (2 * a + c) * 8
                g_src[c, a, :, cols] = out[row : row + 8]
        core_copy(n).start()
        if n > 0:
            pass_on(n - 1)
    pass_on(len(CHUNKS) - 1)
    r2[z] = r2_src[z]
    for n in range(len(CHUNKS)):
        start, width = CHUNKS[n]
        for d in range(3):
            other = others[2 - d]
            arrive_one(far_recv.at[n, other], r2.at[other, :, pl.ds(start, width)])
            far_copy(n, d).wait_send()
    grad_ref[...] = (r2[0] + r2[1]) + (r2[2] + r2[3])
    for phase, buffer in enumerate((s1, ol_all, s2, s3, t1, pen1, t2, pen2, t3, flow_in, direct_in)):
        sent(phase, buffer)


def hand_over(grad_in, pen_in, grad_ref, pen_ref):
    grad_ref[...] = grad_in[...]
    pen_ref[...] = pen_in[...]


def body(injections, transfer_factors, outage_factors, outage_line, limit_table, scenario_tier):
    tile = (8, 256)
    vmem = pltpu.VMEM
    scratch = [
        vmem((1, SCEN), jnp.int32),
        vmem((1, OUTS), jnp.int32),
        vmem((4, ROWS), jnp.int32),
        vmem((ROWS, BUS_COLS), F32),
        vmem((ROWS, BUS_COLS), BF16),
        vmem((ROWS, BUS_COLS), BF16),
        vmem((SCEN, BUS_COLS), F32),
        vmem((2 * SCEN, BUS_COLS), BF16),
        vmem((ROWS, OUTS), F32),
        vmem((OUTS, ROWS), F32),
        vmem((8, 256, 256), BF16),
        vmem((OUTS, 256, 128), F32),
        vmem((256, 128), F32),
        vmem((16, 128, 256), BF16),
        vmem((16, 256, 256), BF16),
        vmem((16,) + tile, F32),
        vmem((16,) + tile, F32),
        vmem(tile, F32),
        vmem((16,) + tile, F32),
        vmem((1, OUTS), F32),
        vmem((16, 1, OUTS), F32),
        vmem((16,) + tile, F32),
        vmem((16,) + tile, F32),
        vmem(tile, F32),
        vmem((16,) + tile, F32),
        vmem((16,) + tile, jnp.int32),
        vmem((16,) + tile, jnp.int32),
        vmem((256, 128), F32),
        vmem((OUTS, 128), F32),
        vmem((256, 128), F32),
        vmem((OUTS, 8, 128), F32),
        vmem((OUTS, 128), F32),
        vmem((8,) + tile, F32),
        vmem((16,) + tile, F32),
        vmem((16,) + tile, F32),
        vmem((16,) + tile, F32),
        vmem((8,) + tile, F32),
        vmem((16,) + tile, F32),
        vmem(tile, F32),
        vmem((16,) + tile, F32),
        vmem((1, 128), F32),
        vmem((16, 1, 128), F32),
        vmem((1, 128), F32),
        vmem((16, 1, 128), F32),
        vmem((2, 4, 8, BUS_COLS), F32),
        vmem((4, 8, BUS_COLS), F32),
        vmem((4, 8, BUS_COLS), F32),
        vmem((4, 8, BUS_COLS), F32),
        pltpu.SemaphoreType.DMA((9,)),
        pltpu.SemaphoreType.DMA((11,)),
        pltpu.SemaphoreType.DMA((11,)),
        pltpu.SemaphoreType.DMA((16,)),
        pltpu.SemaphoreType.DMA((16,)),
        pltpu.SemaphoreType.DMA((5,)),
        pltpu.SemaphoreType.DMA((5,)),
        pltpu.SemaphoreType.DMA((5, 3)),
        pltpu.SemaphoreType.DMA((5, 4)),
    ]
    hbm = pl.BlockSpec(memory_space=pl.ANY)
    whole = pl.BlockSpec(memory_space=pltpu.VMEM)
    grad, penalty = pl.pallas_call(
        kernel,
        out_shape=(
            jax.ShapeDtypeStruct((8, BUS_COLS), F32),
            jax.ShapeDtypeStruct((1, SCEN), F32),
        ),
        in_specs=[hbm] * 6,
        out_specs=(whole, whole),
        scratch_shapes=scratch,
        compiler_params=pltpu.CompilerParams(
            collective_id=0, has_side_effects=True, vmem_limit_bytes=60 << 20
        ),
        name="overload",
    )(
        scenario_tier.reshape(1, SCEN),
        injections,
        transfer_factors,
        outage_factors,
        outage_line.reshape(1, OUTS),
        limit_table,
    )
    grad, penalty = pl.pallas_call(
        hand_over,
        out_shape=(
            jax.ShapeDtypeStruct((8, BUS_COLS), F32),
            jax.ShapeDtypeStruct((1, SCEN), F32),
        ),
        in_specs=[whole, whole],
        out_specs=(whole, whole),
        name="hand_over",
    )(grad, penalty)
    return grad, penalty.reshape(SCEN)


def solution(mesh):
    return jax.shard_map(
        body,
        mesh=mesh,
        in_specs=(
            P(None, "bus"),
            P("line", "bus"),
            P("line", "bus"),
            P("bus"),
            P(None, "line"),
            P(),
        ),
        out_specs=(P("line", "bus"), P()),
        check_vma=False,
    )
```

```python
import jax
import jax.numpy as jnp
from jax import lax
from jax.experimental import pallas as pl
from jax.experimental.pallas import tpu as pltpu
from jax.sharding import PartitionSpec as P

LINES = 4096
OUTAGES = 8192
SCEN = 64
BUS_COLS = 2176
ROWS = 512
OUTS = 256
CHUNKS = ((0, 640), (640, 768), (1408, 768))
F32 = jnp.float32
BF16 = jnp.bfloat16
NT = (((1,), (1,)), ((), ()))


def torus(size, step):
    return min(step, size - step)


PLANE = sorted(
    [(dy, dx) for dy in range(4) for dx in range(4) if dy + dx],
    key=lambda step: -torus(4, step[0]) - torus(4, step[1]),
)
COLUMN = sorted(
    [(dz, dc) for dz in range(8) for dc in range(2) if dz + dc], key=lambda step: -torus(8, step[0])
)


def split(value):
    high = value.astype(BF16)
    return high, (value - high.astype(F32)).astype(BF16)


def kernel(
    tier_hbm, inj_hbm, tf_hbm, w_hbm, ol_hbm, table_hbm, grad_ref, pen_ref,
    tier_ref, ol_ref, table_ref,
    tf, tf_hi, tf_lo, inj, inj_hl, w, w_t, w_parts, w_wide, limit_t, lane_hit, spread_in,
    part, s1, s2_src, s2, ol_src, ol_all, s3_src, s3, flow_src, flow_in, lane_of, tile_of,
    flow_t, outage_t, direct_t, back_rows, back_t,
    t1_src, t1, direct_src, direct_in, t2_src, t2, t3_src, t3, pen_src, pen1, pen2_src, pen2,
    r2_src, r2,
    load_sem, send_sem, recv_sem, near_recv, far_back, t3_recv, pair_sem, far_send, far_recv,
):
    i = lax.axis_index("line")
    j = lax.axis_index("bus")
    p = j // 2
    zh = lax.rem(j, 2)
    q = zh * 8 + i
    core = lax.rem(i, 2)
    z = i // 2
    half = lax.rem(p, 2)

    def plane_peer(step):
        other = lax.rem(p // 4 + step[0], 4) * 4 + lax.rem(p + step[1], 4)
        return other, (i, other * 2 + zh)

    def cross_peer(step):
        other, (line, bus) = plane_peer(step)
        return other, (i + 1 - 2 * core, bus)

    def column_peer(step):
        chip = lax.rem(zh * 4 + z + step[0], 8)
        line = lax.rem(chip, 4) * 2 + lax.rem(core + step[1], 2)
        return (chip // 4) * 8 + line, (line, p * 2 + chip // 4)

    barrier = pltpu.get_barrier_semaphore()

    for peer, steps in ((plane_peer, PLANE), (column_peer, COLUMN), (cross_peer, PLANE)):
        for step in steps:
            pl.semaphore_signal(
                barrier, inc=1, device_id=peer(step)[1], device_id_type=pl.DeviceIdType.MESH
            )
    pairs = [(inj_hbm, inj)]
    pairs += [(tf_hbm.at[pl.ds(n * 128, 128)], tf.at[pl.ds(n * 128, 128)]) for n in range(4)]
    pairs += [(ol_hbm, ol_ref), (w_hbm, w), (table_hbm, table_ref), (tier_hbm, tier_ref)]
    loads = [pltpu.make_async_copy(a, b, load_sem.at[n]) for n, (a, b) in enumerate(pairs)]
    for copy in loads:
        copy.start()

    def send_all(peer, phase, source, target, arrived=None):
        for step in PLANE if peer is plane_peer else COLUMN:
            other, device = peer(step)
            pltpu.make_async_remote_copy(
                src_ref=source(other),
                dst_ref=target,
                send_sem=send_sem.at[phase],
                recv_sem=recv_sem.at[phase] if arrived is None else arrived,
                device_id=device,
                device_id_type=pl.DeviceIdType.MESH,
            ).start()

    def arrive_one(semaphore, view):
        pltpu.make_async_copy(view, view, semaphore).wait()

    def arrive(phase, buffer):
        view = buffer.at[pl.ds(0, 15)]
        pltpu.make_async_copy(view, view, recv_sem.at[phase]).wait()

    def sent(phase, buffer):
        view = buffer.at[pl.ds(0, 15)]
        pltpu.make_async_copy(view, view, send_sem.at[phase]).wait()


    loads[0].wait()
    inj_hi, inj_lo = split(inj[...])
    inj_hl[0:SCEN, :] = inj_hi
    inj_hl[SCEN : 2 * SCEN, :] = inj_lo
    for n in range(2):
        for m in (2 * n, 2 * n + 1):
            loads[1 + m].wait()
        high, low = split(tf[n * 256 : (n + 1) * 256, :])
        rows = pl.ds(pl.multiple_of(core * ROWS + n * 256, 256), 256)
        tf_hi[rows, :] = high
        tf_lo[rows, :] = low
        both = lax.dot_general(inj_hl[...], high, NT, preferred_element_type=F32)
        low = lax.dot_general(inj_hl[0:SCEN, :], low, NT, preferred_element_type=F32)
        flows = both[0:SCEN] + (both[SCEN : 2 * SCEN] + low)
        for group in range(8):
            part[2 * group + n] = flows[group * 8 : (group + 1) * 8]

    key_row = lax.broadcasted_iota(jnp.int32, (256, 256), 0)
    key_col = lax.broadcasted_iota(jnp.int32, (256, 256), 1)
    same_half = jnp.bitwise_and(jnp.right_shift(key_row, 5) - jnp.right_shift(key_col, 6), 1) == 0
    key = jnp.where(same_half, jnp.bitwise_and(key_row, 31) - jnp.right_shift(key_col, 7), -1)

    def widen_start():
        w_t[...] = w[...].T

        def group(g, carry):
            piece = w_t[pl.ds(pl.multiple_of(g * 32, 32), 32), :]
            high = piece.astype(BF16).astype(F32)
            rest = piece - high
            middle = rest.astype(BF16).astype(F32)
            stack = [
                value[:, h * 256 : (h + 1) * 256]
                for value in (high, middle, rest - middle)
                for h in range(2)
            ]
            stack.append(jnp.zeros((64, 256), F32))
            w_parts[g] = jnp.concatenate(stack, axis=0).T.astype(BF16)
            return carry

        lax.fori_loop(0, 8, group, 0)

    def widen(step, carry):
        ones = jnp.where(key == 2 * step, 1.0, 0.0).astype(BF16)
        for g in range(8):
            wide = jnp.dot(w_parts[g], ones, preferred_element_type=F32)
            w_wide[g * 32 + 2 * step] = wide[:, 0:128]
            w_wide[g * 32 + 2 * step + 1] = wide[:, 128:256]
        return carry

    pl.semaphore_wait(barrier, 45)
    send_all(plane_peer, 0, lambda other: part.at[other], s1.at[p])
    loads[5].wait()
    ol_src[...] = ol_ref[...].astype(F32)
    send_all(plane_peer, 1, lambda other: ol_src, ol_all.at[p])
    s1[p] = part[p]
    ol_all[p] = ol_src[...]
    for copy in loads[6:]:
        copy.wait()
    tiers = jnp.concatenate([tier_ref[...], tier_ref[...]], axis=1)
    left = lax.broadcasted_iota(jnp.int32, (128, 128), 1) < SCEN
    for block in range(2):
        rows = slice(block * 128, (block + 1) * 128)
        value = jnp.zeros((128, 128), F32)
        for tier in range(4):
            pair = [
                jnp.broadcast_to(
                    0.4 * table_ref[tier : tier + 1, h * 256 + block * 128 : h * 256 + block * 128 + 128].astype(F32),
                    (128, 128),
                ).T
                for h in range(2)
            ]
            value = jnp.where(tiers == tier, jnp.where(left, pair[0], pair[1]), value)
        limit_t[rows, :] = value
    widen_start()
    lax.fori_loop(0, 2, widen, 0)
    arrive(0, s1)
    s2_src[...] = jnp.sum(s1[...], axis=0)
    send_all(column_peer, 2, lambda other: s2_src, s2.at[q], near_recv.at[q])
    s2[q] = s2_src[...]
    arrive(1, ol_all)

    lax.fori_loop(2, 7, widen, 0)
    def names(group, carry):
        where = jnp.broadcast_to(ol_all[group], (8, 256)).astype(jnp.int32)
        lane_of[group] = jnp.bitwise_and(where, 127)
        tile_of[group] = jnp.right_shift(where, 7)
        return carry

    lax.fori_loop(0, 16, names, 0)
    for ahead in (2, 1, 3, 0):
        blocks = [lax.rem(z + ahead, 4) * 2 + c for c in range(2)]
        sources = []
        for block in blocks:
            for h in range(2):
                slot = h * 8 + block

                @pl.when(slot != q)
                def _():
                    arrive_one(near_recv.at[slot], s2.at[slot])

            full = s2[block] + s2[8 + block]
            for k in range(2):
                sources.append((block * 4 + 2 * half + k, full[:, k * 128 : (k + 1) * 128]))
        for group in range(16):
            for k in range(2):
                cols = slice(k * 128, (k + 1) * 128)
                lane = lane_of[group, :, cols]
                tile = tile_of[group, :, cols]
                out = jnp.zeros((8, 128), F32) if ahead == 2 else s3_src[group, :, cols]
                for name, source in sources:
                    out = jnp.where(tile == name, jnp.take_along_axis(source, lane, axis=1), out)
                s3_src[group, :, cols] = out
    flow_src[...] = s2[i] + s2[8 + i]
    send_all(plane_peer, 3, lambda other: s3_src.at[other], s3.at[p])
    send_all(plane_peer, 9, lambda other: flow_src, flow_in.at[p])
    s3[p] = s3_src[p]
    flow_in[p] = flow_src[...]
    lax.fori_loop(7, 16, widen, 0)
    arrive(3, s3)
    arrive(9, flow_in)
    tiles = jnp.concatenate([flow_in[2 * g + h] for h in range(2) for g in range(8)], axis=0)
    flow_t[...] = tiles.T
    picked = jnp.concatenate([s3[2 * g] + s3[2 * g + 1] for g in range(8)], axis=0)
    outage_t[...] = jnp.concatenate([picked, picked], axis=0).T

    pair = pltpu.make_async_remote_copy(
        src_ref=tf_hbm,
        dst_ref=tf,
        send_sem=pair_sem.at[0],
        recv_sem=pair_sem.at[1],
        device_id=(i + 1 - 2 * core, j),
        device_id_type=pl.DeviceIdType.MESH,
    )
    pair.start()

    penalty = jnp.zeros((8, 128), F32)
    for block in range(4):
        slabs = [slice(block * 64 + v * 8, block * 64 + v * 8 + 8) for v in range(8)]
        flow = [flow_t[rows, :] for rows in slabs]
        top = [limit_t[rows, :] for rows in slabs]
        low = [-value for value in top]

        def outages(step, carry):
            direct = list(carry[:8])
            squares = carry[8]
            eight = pl.ds(pl.multiple_of(step * 8, 8), 8)
            near = outage_t[eight, :]
            sums = []
            for u in range(8):
                name = step * 8 + u
                here = jnp.broadcast_to(near[u : u + 1, :], (8, 128))
                back = None
                for v in range(8):
                    factor = w_wide[name, slabs[v], :]
                    post = factor * here + flow[v]
                    over = post - jnp.minimum(jnp.maximum(post, low[v]), top[v])
                    direct[v] = direct[v] + over
                    term = over * factor
                    back = term if back is None else back + term
                    squares = squares + over * over
                if block > 0:
                    back = back + back_rows[name]
                if block < 3:
                    back_rows[name] = back
                else:
                    sums.append(jnp.sum(back, axis=0, keepdims=True))
            if block == 3:
                back_t[eight, :] = jnp.concatenate(sums, axis=0)
            return tuple(direct) + (squares,)

        start = tuple(jnp.zeros((8, 128), F32) for _ in range(8)) + (penalty,)
        result = lax.fori_loop(0, 32, outages, start)
        for v in range(8):
            direct_t[slabs[v], :] = result[v]
        penalty = result[8]

    back = back_t[...].T
    back = back[0:SCEN] + back[SCEN : 2 * SCEN]
    for g in range(8):
        t1_src[g] = back[g * 8 : (g + 1) * 8, :]
    send_all(plane_peer, 4, lambda other: t1_src.at[other // 2], t1.at[p], far_back.at[p])
    t1[p] = t1_src[p // 2]
    direct = direct_t[...].T
    for h in range(2):
        for g in range(8):
            direct_src[2 * g + h] = direct[h * SCEN + g * 8 : h * SCEN + g * 8 + 8, :]
    send_all(plane_peer, 10, lambda other: direct_src.at[other], direct_in.at[p])
    direct_in[p] = direct_src[p]
    pen_src[...] = jnp.sum(penalty, axis=0, keepdims=True)
    send_all(plane_peer, 5, lambda other: pen_src, pen1.at[p])
    pen1[p] = pen_src[...]
    def mark(group, carry):
        lane = jnp.bitwise_and(jnp.broadcast_to(ol_all[group], (128, 256)).astype(jnp.int32), 127)
        hit = lane == lax.broadcasted_iota(jnp.int32, (128, 256), 0)
        lane_hit[group] = jnp.where(hit, 1.0, 0.0).astype(BF16)
        return carry

    lax.fori_loop(0, 16, mark, 0)
    pair.wait()

    def cut(step, carry):
        rows = pl.ds(pl.multiple_of(step * 64, 64), 64)
        high, low = split(tf[rows, :])
        rows = pl.ds(pl.multiple_of((1 - core) * ROWS + step * 64, 64), 64)
        tf_hi[rows, :] = high
        tf_lo[rows, :] = low
        return carry

    lax.fori_loop(0, 8, cut, 0)

    total = jnp.zeros((256, 128), F32)
    for turn, step in enumerate([(0, 0)] + PLANE[::-1]):
        group = plane_peer(step)[0]
        if step != (0, 0):
            arrive_one(far_back.at[group], t1.at[group])
        high, low = split(t1[group])
        both = jnp.concatenate([high.astype(F32), low.astype(F32)], axis=0)
        tile = jnp.concatenate([tile_of[group], tile_of[group]], axis=0) - 2 * half
        for t in range(16):
            name = (t // 2) * 4 + t % 2
            spread_in[turn % 4, t * 16 : (t + 1) * 16, :] = jnp.where(tile == name, both, 0.0).astype(BF16)
        total = total + lax.dot_general(
            spread_in[turn % 4], lane_hit[group], NT, preferred_element_type=F32
        )
    for t in range(16):
        cols = slice((t % 2) * 128, (t % 2) * 128 + 128)
        t2_src[t // 2, :, cols] = total[t * 16 : t * 16 + 8] + total[t * 16 + 8 : t * 16 + 16]
    arrive(10, direct_in)
    t2_src[i] = t2_src[i] + jnp.sum(direct_in[...], axis=0)
    send_all(column_peer, 6, lambda other: t2_src.at[lax.rem(other, 8)], t2.at[q])
    t2[q] = t2_src[i]
    arrive(5, pen1)
    pen2_src[...] = jnp.sum(pen1[...], axis=0)
    send_all(column_peer, 7, lambda other: pen2_src, pen2.at[q])
    pen2[q] = pen2_src[...]
    arrive(6, t2)
    t3_src[...] = jnp.sum(t2[...], axis=0) * (2.0 / OUTAGES)
    target = lax.rem(p // 2, 2)
    slot = core * 8 + (p // 4) * 2 + half

    def hand(step):
        other = plane_peer(step)[0]
        return pltpu.make_async_remote_copy(
            src_ref=t3_src,
            dst_ref=t3.at[slot],
            send_sem=send_sem.at[8],
            recv_sem=t3_recv.at[slot],
            device_id=(z * 2 + target, other * 2 + zh),
            device_id_type=pl.DeviceIdType.MESH,
        )

    for step in PLANE:
        hand(step).start()

    @pl.when(target != core)
    def _():
        hand((0, 0)).start()

    @pl.when(target == core)
    def _():
        t3[slot] = t3_src[...]

    arrive(7, pen2)
    both = jnp.sum(pen2[...], axis=0) * (1.0 / (LINES * OUTAGES))
    pen_ref[...] = both[:, 0:SCEN] + both[:, SCEN:128]
    for n in range(16):

        @pl.when(jnp.logical_or(slot != n, target != core))
        def _():
            arrive_one(t3_recv.at[n], t3.at[n])

    grad = jnp.concatenate(
        [
            jnp.concatenate([t3[c * 8 + a * 2 + h] for a in range(4)], axis=0)
            for c in range(2)
            for h in range(2)
        ],
        axis=1,
    )
    grad_hi, grad_lo = split(grad)
    grad_hl = jnp.concatenate([grad_hi, grad_lo], axis=0)
    right = z // 2
    others = (3 - 3 * right, 2 - right, z + 1 - 2 * lax.rem(z, 2))

    def far_copy(n, d):
        start, width = CHUNKS[n]
        cols = pl.ds(start, width)
        return pltpu.make_async_remote_copy(
            src_ref=r2_src.at[others[d], :, cols],
            dst_ref=r2.at[z, :, cols],
            send_sem=far_send.at[n, d],
            recv_sem=far_recv.at[n, z],
            device_id=(others[d] * 2 + core, j),
            device_id_type=pl.DeviceIdType.MESH,
        )

    for n, (start, width) in enumerate(CHUNKS):
        cols = slice(start, start + width)
        both = jnp.dot(grad_hl, tf_hi[:, cols], preferred_element_type=F32)
        low = jnp.dot(grad_hi, tf_lo[:, cols], preferred_element_type=F32)
        out = both[0:32] + (both[32:64] + low)
        for a in range(4):
            r2_src[a, :, cols] = out[a * 8 : (a + 1) * 8]
        for d in range(2):
            far_copy(n, d).start()
    for n in range(len(CHUNKS)):
        far_copy(n, 2).start()
    r2[z] = r2_src[z]
    for n in range(len(CHUNKS)):
        start, width = CHUNKS[n]
        for d in range(3):
            other = others[2 - d]
            arrive_one(far_recv.at[n, other], r2.at[other, :, pl.ds(start, width)])
            far_copy(n, d).wait_send()
    grad_ref[...] = (r2[0] + r2[1]) + (r2[2] + r2[3])
    for phase, buffer in enumerate((s1, ol_all, s2, s3, t1, pen1, t2, pen2, t3, flow_in, direct_in)):
        sent(phase, buffer)

    @pl.when(target != core)
    def _():
        arrive_one(send_sem.at[8], t3.at[0])


def hand_over(grad_in, pen_in, grad_ref, pen_ref):
    grad_ref[...] = grad_in[...]
    pen_ref[...] = pen_in[...]


def body(injections, transfer_factors, outage_factors, outage_line, limit_table, scenario_tier):
    tile = (8, 256)
    vmem = pltpu.VMEM
    scratch = [
        vmem((1, SCEN), jnp.int32),
        vmem((1, OUTS), jnp.int32),
        vmem((4, ROWS), jnp.int32),
        vmem((ROWS, BUS_COLS), F32),
        vmem((2 * ROWS, BUS_COLS), BF16),
        vmem((2 * ROWS, BUS_COLS), BF16),
        vmem((SCEN, BUS_COLS), F32),
        vmem((2 * SCEN, BUS_COLS), BF16),
        vmem((ROWS, OUTS), F32),
        vmem((OUTS, ROWS), F32),
        vmem((8, 256, 256), BF16),
        vmem((OUTS, 256, 128), F32),
        vmem((256, 128), F32),
        vmem((16, 128, 256), BF16),
        vmem((4, 256, 256), BF16),
        vmem((16,) + tile, F32),
        vmem((16,) + tile, F32),
        vmem(tile, F32),
        vmem((16,) + tile, F32),
        vmem((1, OUTS), F32),
        vmem((16, 1, OUTS), F32),
        vmem((16,) + tile, F32),
        vmem((16,) + tile, F32),
        vmem(tile, F32),
        vmem((16,) + tile, F32),
        vmem((16,) + tile, jnp.int32),
        vmem((16,) + tile, jnp.int32),
        vmem((256, 128), F32),
        vmem((OUTS, 128), F32),
        vmem((256, 128), F32),
        vmem((OUTS, 8, 128), F32),
        vmem((OUTS, 128), F32),
        vmem((8,) + tile, F32),
        vmem((16,) + tile, F32),
        vmem((16,) + tile, F32),
        vmem((16,) + tile, F32),
        vmem((8,) + tile, F32),
        vmem((16,) + tile, F32),
        vmem(tile, F32),
        vmem((16,) + tile, F32),
        vmem((1, 128), F32),
        vmem((16, 1, 128), F32),
        vmem((1, 128), F32),
        vmem((16, 1, 128), F32),
        vmem((4, 8, BUS_COLS), F32),
        vmem((4, 8, BUS_COLS), F32),
        pltpu.SemaphoreType.DMA((9,)),
        pltpu.SemaphoreType.DMA((11,)),
        pltpu.SemaphoreType.DMA((11,)),
        pltpu.SemaphoreType.DMA((16,)),
        pltpu.SemaphoreType.DMA((16,)),
        pltpu.SemaphoreType.DMA((16,)),
        pltpu.SemaphoreType.DMA((2,)),
        pltpu.SemaphoreType.DMA((3, 3)),
        pltpu.SemaphoreType.DMA((3, 4)),
    ]
    hbm = pl.BlockSpec(memory_space=pl.ANY)
    whole = pl.BlockSpec(memory_space=pltpu.VMEM)
    grad, penalty = pl.pallas_call(
        kernel,
        out_shape=(
            jax.ShapeDtypeStruct((8, BUS_COLS), F32),
            jax.ShapeDtypeStruct((1, SCEN), F32),
        ),
        in_specs=[hbm] * 6,
        out_specs=(whole, whole),
        scratch_shapes=scratch,
        compiler_params=pltpu.CompilerParams(
            collective_id=0, has_side_effects=True, vmem_limit_bytes=60 << 20
        ),
        name="overload",
    )(
        scenario_tier.reshape(1, SCEN),
        injections,
        transfer_factors,
        outage_factors,
        outage_line.reshape(1, OUTS),
        limit_table,
    )
    grad, penalty = pl.pallas_call(
        hand_over,
        out_shape=(
            jax.ShapeDtypeStruct((8, BUS_COLS), F32),
            jax.ShapeDtypeStruct((1, SCEN), F32),
        ),
        in_specs=[whole, whole],
        out_specs=(whole, whole),
        name="hand_over",
    )(grad, penalty)
    return grad, penalty.reshape(SCEN)


def solution(mesh):
    return jax.shard_map(
        body,
        mesh=mesh,
        in_specs=(
            P(None, "bus"),
            P("line", "bus"),
            P("line", "bus"),
            P("bus"),
            P(None, "line"),
            P(),
        ),
        out_specs=(P("line", "bus"), P()),
        check_vma=False,
    )
```

```python
import jax
import jax.numpy as jnp
from jax import lax
from jax.experimental import pallas as pl
from jax.experimental.pallas import tpu as pltpu
from jax.sharding import PartitionSpec as P

LINES = 4096
OUTAGES = 8192
SCEN = 64
BUS_COLS = 2176
ROWS = 512
OUTS = 256
CHUNKS = ((0, 640), (640, 768), (1408, 768))
F32 = jnp.float32
BF16 = jnp.bfloat16
NT = (((1,), (1,)), ((), ()))


def torus(size, step):
    return min(step, size - step)


PLANE = sorted(
    [(dy, dx) for dy in range(4) for dx in range(4) if dy + dx],
    key=lambda step: -torus(4, step[0]) - torus(4, step[1]),
)
COLUMN = sorted(
    [(dz, dc) for dz in range(8) for dc in range(2) if dz + dc], key=lambda step: -torus(8, step[0])
)


def split(value):
    high = value.astype(BF16)
    return high, (value - high.astype(F32)).astype(BF16)


def kernel(
    tier_hbm, inj_hbm, tf_hbm, w_hbm, ol_hbm, table_hbm, grad_ref, pen_ref,
    tier_ref, ol_ref, table_ref,
    tf, tf_hi, tf_lo, inj, inj_hl, w, w_t, w_parts, w_wide, limit_t, lane_hit, spread_in,
    part, s1, s2_src, s2, ol_src, ol_all, s3_src, s3, flow_src, flow_in, lane_of, tile_of,
    flow_t, outage_t, direct_t, back_rows, back_t,
    t1_src, t1, direct_src, direct_in, t2_src, t2, t3_src, t3, pen_src, pen1, pen2_src, pen2,
    r2_src, r2,
    load_sem, send_sem, recv_sem, near_recv, far_back, t3_recv, pair_sem, far_send, far_recv,
):
    i = lax.axis_index("line")
    j = lax.axis_index("bus")
    p = j // 2
    zh = lax.rem(j, 2)
    q = zh * 8 + i
    core = lax.rem(i, 2)
    z = i // 2
    half = lax.rem(p, 2)

    def plane_peer(step):
        other = lax.rem(p // 4 + step[0], 4) * 4 + lax.rem(p + step[1], 4)
        return other, (i, other * 2 + zh)

    def cross_peer(step):
        other, (line, bus) = plane_peer(step)
        return other, (i + 1 - 2 * core, bus)

    def column_peer(step):
        chip = lax.rem(zh * 4 + z + step[0], 8)
        line = lax.rem(chip, 4) * 2 + lax.rem(core + step[1], 2)
        return (chip // 4) * 8 + line, (line, p * 2 + chip // 4)

    barrier = pltpu.get_barrier_semaphore()

    for peer, steps in ((plane_peer, PLANE), (column_peer, COLUMN), (cross_peer, PLANE)):
        for step in steps:
            pl.semaphore_signal(
                barrier, inc=1, device_id=peer(step)[1], device_id_type=pl.DeviceIdType.MESH
            )
    pairs = [(inj_hbm, inj)]
    pairs += [(tf_hbm.at[pl.ds(n * 128, 128)], tf.at[pl.ds(n * 128, 128)]) for n in range(4)]
    pairs += [(ol_hbm, ol_ref), (w_hbm, w), (table_hbm, table_ref), (tier_hbm, tier_ref)]
    loads = [pltpu.make_async_copy(a, b, load_sem.at[n]) for n, (a, b) in enumerate(pairs)]
    for copy in loads:
        copy.start()

    def send_all(peer, phase, source, target, arrived=None):
        for step in PLANE if peer is plane_peer else COLUMN:
            other, device = peer(step)
            pltpu.make_async_remote_copy(
                src_ref=source(other),
                dst_ref=target,
                send_sem=send_sem.at[phase],
                recv_sem=recv_sem.at[phase] if arrived is None else arrived,
                device_id=device,
                device_id_type=pl.DeviceIdType.MESH,
            ).start()

    def arrive_one(semaphore, view):
        pltpu.make_async_copy(view, view, semaphore).wait()

    def arrive(phase, buffer):
        view = buffer.at[pl.ds(0, 15)]
        pltpu.make_async_copy(view, view, recv_sem.at[phase]).wait()

    def sent(phase, buffer):
        view = buffer.at[pl.ds(0, 15)]
        pltpu.make_async_copy(view, view, send_sem.at[phase]).wait()


    loads[0].wait()
    inj_hi, inj_lo = split(inj[...])
    inj_hl[0:SCEN, :] = inj_hi
    inj_hl[SCEN : 2 * SCEN, :] = inj_lo
    for n in range(2):
        for m in (2 * n, 2 * n + 1):
            loads[1 + m].wait()
        high, low = split(tf[n * 256 : (n + 1) * 256, :])
        rows = pl.ds(pl.multiple_of(core * ROWS + n * 256, 256), 256)
        tf_hi[rows, :] = high
        tf_lo[rows, :] = low
        both = lax.dot_general(inj_hl[...], high, NT, preferred_element_type=F32)
        low = lax.dot_general(inj_hl[0:SCEN, :], low, NT, preferred_element_type=F32)
        flows = both[0:SCEN] + (both[SCEN : 2 * SCEN] + low)
        for group in range(8):
            part[2 * group + n] = flows[group * 8 : (group + 1) * 8]

    key_row = lax.broadcasted_iota(jnp.int32, (256, 256), 0)
    key_col = lax.broadcasted_iota(jnp.int32, (256, 256), 1)
    same_half = jnp.bitwise_and(jnp.right_shift(key_row, 5) - jnp.right_shift(key_col, 6), 1) == 0
    key = jnp.where(same_half, jnp.bitwise_and(key_row, 31) - jnp.right_shift(key_col, 7), -1)

    def widen_start():
        w_t[...] = w[...].T

        def group(g, carry):
            piece = w_t[pl.ds(pl.multiple_of(g * 32, 32), 32), :]
            high = piece.astype(BF16).astype(F32)
            rest = piece - high
            middle = rest.astype(BF16).astype(F32)
            stack = [
                value[:, h * 256 : (h + 1) * 256]
                for value in (high, middle, rest - middle)
                for h in range(2)
            ]
            stack.append(jnp.zeros((64, 256), F32))
            w_parts[g] = jnp.concatenate(stack, axis=0).T.astype(BF16)
            return carry

        lax.fori_loop(0, 8, group, 0)

    def widen(step, carry):
        ones = jnp.where(key == 2 * step, 1.0, 0.0).astype(BF16)
        for g in range(8):
            wide = jnp.dot(w_parts[g], ones, preferred_element_type=F32)
            w_wide[g * 32 + 2 * step] = wide[:, 0:128]
            w_wide[g * 32 + 2 * step + 1] = wide[:, 128:256]
        return carry

    pl.semaphore_wait(barrier, 45)
    send_all(plane_peer, 0, lambda other: part.at[other], s1.at[p])
    loads[5].wait()
    ol_src[...] = ol_ref[...].astype(F32)
    send_all(plane_peer, 1, lambda other: ol_src, ol_all.at[p])
    s1[p] = part[p]
    ol_all[p] = ol_src[...]
    for copy in loads[6:]:
        copy.wait()
    tiers = jnp.concatenate([tier_ref[...], tier_ref[...]], axis=1)
    left = lax.broadcasted_iota(jnp.int32, (128, 128), 1) < SCEN
    for block in range(2):
        rows = slice(block * 128, (block + 1) * 128)
        value = jnp.zeros((128, 128), F32)
        for tier in range(4):
            pair = [
                jnp.broadcast_to(
                    0.4 * table_ref[tier : tier + 1, h * 256 + block * 128 : h * 256 + block * 128 + 128].astype(F32),
                    (128, 128),
                ).T
                for h in range(2)
            ]
            value = jnp.where(tiers == tier, jnp.where(left, pair[0], pair[1]), value)
        limit_t[rows, :] = value
    widen_start()
    lax.fori_loop(0, 3, widen, 0)
    arrive(0, s1)
    s2_src[...] = jnp.sum(s1[...], axis=0)
    send_all(column_peer, 2, lambda other: s2_src, s2.at[q], near_recv.at[q])
    s2[q] = s2_src[...]
    arrive(1, ol_all)

    lax.fori_loop(3, 9, widen, 0)
    def names(group, carry):
        where = jnp.broadcast_to(ol_all[group], (8, 256)).astype(jnp.int32)
        lane_of[group] = jnp.bitwise_and(where, 127)
        tile_of[group] = jnp.right_shift(where, 7)
        return carry

    lax.fori_loop(0, 16, names, 0)
    for ahead in (2, 1, 3, 0):
        blocks = [lax.rem(z + ahead, 4) * 2 + c for c in range(2)]
        sources = []
        for block in blocks:
            for h in range(2):
                slot = h * 8 + block

                @pl.when(slot != q)
                def _():
                    arrive_one(near_recv.at[slot], s2.at[slot])

            full = s2[block] + s2[8 + block]
            for k in range(2):
                sources.append((block * 4 + 2 * half + k, full[:, k * 128 : (k + 1) * 128]))
        for group in range(16):
            for k in range(2):
                cols = slice(k * 128, (k + 1) * 128)
                lane = lane_of[group, :, cols]
                tile = tile_of[group, :, cols]
                out = jnp.zeros((8, 128), F32) if ahead == 2 else s3_src[group, :, cols]
                for name, source in sources:
                    out = jnp.where(tile == name, jnp.take_along_axis(source, lane, axis=1), out)
                s3_src[group, :, cols] = out
    flow_src[...] = s2[i] + s2[8 + i]
    send_all(plane_peer, 3, lambda other: s3_src.at[other], s3.at[p])
    send_all(plane_peer, 9, lambda other: flow_src, flow_in.at[p])
    s3[p] = s3_src[p]
    flow_in[p] = flow_src[...]
    lax.fori_loop(9, 16, widen, 0)
    arrive(3, s3)
    arrive(9, flow_in)
    tiles = jnp.concatenate([flow_in[2 * g + h] for h in range(2) for g in range(8)], axis=0)
    flow_t[...] = tiles.T
    picked = jnp.concatenate([s3[2 * g] + s3[2 * g + 1] for g in range(8)], axis=0)
    outage_t[...] = jnp.concatenate([picked, picked], axis=0).T

    pair = pltpu.make_async_remote_copy(
        src_ref=tf_hbm,
        dst_ref=tf,
        send_sem=pair_sem.at[0],
        recv_sem=pair_sem.at[1],
        device_id=(i + 1 - 2 * core, j),
        device_id_type=pl.DeviceIdType.MESH,
    )
    pair.start()

    penalty = [jnp.zeros((8, 128), F32)] * 4
    for block in range(4):
        slabs = [slice(block * 64 + v * 8, block * 64 + v * 8 + 8) for v in range(8)]
        flow = [flow_t[rows, :] for rows in slabs]
        top = [limit_t[rows, :] for rows in slabs]
        low = [-value for value in top]

        def outages(step, carry):
            direct = list(carry[:8])
            squares = list(carry[8:])
            eight = pl.ds(pl.multiple_of(step * 8, 8), 8)
            near = outage_t[eight, :]
            sums = []
            for u in range(8):
                name = step * 8 + u
                here = jnp.broadcast_to(near[u : u + 1, :], (8, 128))
                back = None
                for v in range(8):
                    factor = w_wide[name, slabs[v], :]
                    post = factor * here + flow[v]
                    over = post - jnp.minimum(jnp.maximum(post, low[v]), top[v])
                    direct[v] = direct[v] + over
                    term = over * factor
                    back = term if back is None else back + term
                    squares[v % 4] = squares[v % 4] + over * over
                if block > 0:
                    back = back + back_rows[name]
                if block < 3:
                    back_rows[name] = back
                else:
                    sums.append(jnp.sum(back, axis=0, keepdims=True))
            if block == 3:
                back_t[eight, :] = jnp.concatenate(sums, axis=0)
            return tuple(direct) + tuple(squares)

        start = tuple(jnp.zeros((8, 128), F32) for _ in range(8)) + tuple(penalty)
        result = lax.fori_loop(0, 32, outages, start)
        for v in range(8):
            direct_t[slabs[v], :] = result[v]
        penalty = result[8:]

    back = back_t[...].T
    back = back[0:SCEN] + back[SCEN : 2 * SCEN]
    for g in range(8):
        t1_src[g] = back[g * 8 : (g + 1) * 8, :]
    send_all(plane_peer, 4, lambda other: t1_src.at[other // 2], t1.at[p], far_back.at[p])
    t1[p] = t1_src[p // 2]
    direct = direct_t[...].T
    for h in range(2):
        for g in range(8):
            direct_src[2 * g + h] = direct[h * SCEN + g * 8 : h * SCEN + g * 8 + 8, :]
    send_all(plane_peer, 10, lambda other: direct_src.at[other], direct_in.at[p])
    direct_in[p] = direct_src[p]
    squares = (penalty[0] + penalty[1]) + (penalty[2] + penalty[3])
    pen_src[...] = jnp.sum(squares, axis=0, keepdims=True)
    send_all(plane_peer, 5, lambda other: pen_src, pen1.at[p])
    pen1[p] = pen_src[...]
    def mark(group, carry):
        lane = jnp.bitwise_and(jnp.broadcast_to(ol_all[group], (128, 256)).astype(jnp.int32), 127)
        hit = lane == lax.broadcasted_iota(jnp.int32, (128, 256), 0)
        lane_hit[group] = jnp.where(hit, 1.0, 0.0).astype(BF16)
        return carry

    lax.fori_loop(0, 16, mark, 0)
    pair.wait()

    def cut(step, carry):
        rows = pl.ds(pl.multiple_of(step * 64, 64), 64)
        high, low = split(tf[rows, :])
        rows = pl.ds(pl.multiple_of((1 - core) * ROWS + step * 64, 64), 64)
        tf_hi[rows, :] = high
        tf_lo[rows, :] = low
        return carry

    lax.fori_loop(0, 8, cut, 0)

    total = jnp.zeros((256, 128), F32)
    for turn, step in enumerate([(0, 0)] + PLANE[::-1]):
        group = plane_peer(step)[0]
        if step != (0, 0):
            arrive_one(far_back.at[group], t1.at[group])
        high, low = split(t1[group])
        both = jnp.concatenate([high.astype(F32), low.astype(F32)], axis=0)
        tile = jnp.concatenate([tile_of[group], tile_of[group]], axis=0) - 2 * half
        for t in range(16):
            name = (t // 2) * 4 + t % 2
            spread_in[turn % 4, t * 16 : (t + 1) * 16, :] = jnp.where(tile == name, both, 0.0).astype(BF16)
        total = total + lax.dot_general(
            spread_in[turn % 4], lane_hit[group], NT, preferred_element_type=F32
        )
    for t in range(16):
        cols = slice((t % 2) * 128, (t % 2) * 128 + 128)
        t2_src[t // 2, :, cols] = total[t * 16 : t * 16 + 8] + total[t * 16 + 8 : t * 16 + 16]
    arrive(10, direct_in)
    t2_src[i] = t2_src[i] + jnp.sum(direct_in[...], axis=0)
    send_all(column_peer, 6, lambda other: t2_src.at[lax.rem(other, 8)], t2.at[q])
    t2[q] = t2_src[i]
    arrive(5, pen1)
    pen2_src[...] = jnp.sum(pen1[...], axis=0)
    send_all(column_peer, 7, lambda other: pen2_src, pen2.at[q])
    pen2[q] = pen2_src[...]
    arrive(6, t2)
    t3_src[...] = jnp.sum(t2[...], axis=0) * (2.0 / OUTAGES)
    target = lax.rem(p // 2, 2)
    slot = core * 8 + (p // 4) * 2 + half

    def hand(step):
        other = plane_peer(step)[0]
        return pltpu.make_async_remote_copy(
            src_ref=t3_src,
            dst_ref=t3.at[slot],
            send_sem=send_sem.at[8],
            recv_sem=t3_recv.at[slot],
            device_id=(z * 2 + target, other * 2 + zh),
            device_id_type=pl.DeviceIdType.MESH,
        )

    for step in PLANE:
        hand(step).start()

    @pl.when(target != core)
    def _():
        hand((0, 0)).start()

    @pl.when(target == core)
    def _():
        t3[slot] = t3_src[...]

    arrive(7, pen2)
    both = jnp.sum(pen2[...], axis=0) * (1.0 / (LINES * OUTAGES))
    pen_ref[...] = both[:, 0:SCEN] + both[:, SCEN:128]
    for n in range(16):

        @pl.when(jnp.logical_or(slot != n, target != core))
        def _():
            arrive_one(t3_recv.at[n], t3.at[n])

    grad = jnp.concatenate(
        [
            jnp.concatenate([t3[c * 8 + a * 2 + h] for a in range(4)], axis=0)
            for c in range(2)
            for h in range(2)
        ],
        axis=1,
    )
    grad_hi, grad_lo = split(grad)
    grad_hl = jnp.concatenate([grad_hi, grad_lo], axis=0)
    right = z // 2
    others = (3 - 3 * right, 2 - right, z + 1 - 2 * lax.rem(z, 2))

    def far_copy(n, d):
        start, width = CHUNKS[n]
        cols = pl.ds(start, width)
        return pltpu.make_async_remote_copy(
            src_ref=r2_src.at[others[d], :, cols],
            dst_ref=r2.at[z, :, cols],
            send_sem=far_send.at[n, d],
            recv_sem=far_recv.at[n, z],
            device_id=(others[d] * 2 + core, j),
            device_id_type=pl.DeviceIdType.MESH,
        )

    for n, (start, width) in enumerate(CHUNKS):
        cols = slice(start, start + width)
        both = jnp.dot(grad_hl, tf_hi[:, cols], preferred_element_type=F32)
        low = jnp.dot(grad_hi, tf_lo[:, cols], preferred_element_type=F32)
        out = both[0:32] + (both[32:64] + low)
        for a in range(4):
            r2_src[a, :, cols] = out[a * 8 : (a + 1) * 8]
        for d in range(2):
            far_copy(n, d).start()
    for n in range(len(CHUNKS)):
        far_copy(n, 2).start()
    r2[z] = r2_src[z]
    for n in range(len(CHUNKS)):
        start, width = CHUNKS[n]
        for d in range(3):
            other = others[2 - d]
            arrive_one(far_recv.at[n, other], r2.at[other, :, pl.ds(start, width)])
            far_copy(n, d).wait_send()
    grad_ref[...] = (r2[0] + r2[1]) + (r2[2] + r2[3])
    for phase, buffer in enumerate((s1, ol_all, s2, s3, t1, pen1, t2, pen2, t3, flow_in, direct_in)):
        sent(phase, buffer)

    @pl.when(target != core)
    def _():
        arrive_one(send_sem.at[8], t3.at[0])


def body(injections, transfer_factors, outage_factors, outage_line, limit_table, scenario_tier):
    tile = (8, 256)
    vmem = pltpu.VMEM
    scratch = [
        vmem((1, SCEN), jnp.int32),
        vmem((1, OUTS), jnp.int32),
        vmem((4, ROWS), jnp.int32),
        vmem((ROWS, BUS_COLS), F32),
        vmem((2 * ROWS, BUS_COLS), BF16),
        vmem((2 * ROWS, BUS_COLS), BF16),
        vmem((SCEN, BUS_COLS), F32),
        vmem((2 * SCEN, BUS_COLS), BF16),
        vmem((ROWS, OUTS), F32),
        vmem((OUTS, ROWS), F32),
        vmem((8, 256, 256), BF16),
        vmem((OUTS, 256, 128), F32),
        vmem((256, 128), F32),
        vmem((16, 128, 256), BF16),
        vmem((4, 256, 256), BF16),
        vmem((16,) + tile, F32),
        vmem((16,) + tile, F32),
        vmem(tile, F32),
        vmem((16,) + tile, F32),
        vmem((1, OUTS), F32),
        vmem((16, 1, OUTS), F32),
        vmem((16,) + tile, F32),
        vmem((16,) + tile, F32),
        vmem(tile, F32),
        vmem((16,) + tile, F32),
        vmem((16,) + tile, jnp.int32),
        vmem((16,) + tile, jnp.int32),
        vmem((256, 128), F32),
        vmem((OUTS, 128), F32),
        vmem((256, 128), F32),
        vmem((OUTS, 8, 128), F32),
        vmem((OUTS, 128), F32),
        vmem((8,) + tile, F32),
        vmem((16,) + tile, F32),
        vmem((16,) + tile, F32),
        vmem((16,) + tile, F32),
        vmem((8,) + tile, F32),
        vmem((16,) + tile, F32),
        vmem(tile, F32),
        vmem((16,) + tile, F32),
        vmem((1, 128), F32),
        vmem((16, 1, 128), F32),
        vmem((1, 128), F32),
        vmem((16, 1, 128), F32),
        vmem((4, 8, BUS_COLS), F32),
        vmem((4, 8, BUS_COLS), F32),
        pltpu.SemaphoreType.DMA((9,)),
        pltpu.SemaphoreType.DMA((11,)),
        pltpu.SemaphoreType.DMA((11,)),
        pltpu.SemaphoreType.DMA((16,)),
        pltpu.SemaphoreType.DMA((16,)),
        pltpu.SemaphoreType.DMA((16,)),
        pltpu.SemaphoreType.DMA((2,)),
        pltpu.SemaphoreType.DMA((3, 3)),
        pltpu.SemaphoreType.DMA((3, 4)),
    ]
    hbm = pl.BlockSpec(memory_space=pl.ANY)
    whole = pl.BlockSpec(memory_space=pltpu.VMEM)
    grad, penalty = pl.pallas_call(
        kernel,
        out_shape=(
            pltpu.VMEM((8, BUS_COLS), F32),
            pltpu.VMEM((1, SCEN), F32),
        ),
        in_specs=[hbm] * 6,
        out_specs=(whole, whole),
        scratch_shapes=scratch,
        compiler_params=pltpu.CompilerParams(
            collective_id=0, has_side_effects=True, vmem_limit_bytes=60 << 20
        ),
        name="overload",
    )(
        scenario_tier.reshape(1, SCEN),
        injections,
        transfer_factors,
        outage_factors,
        outage_line.reshape(1, OUTS),
        limit_table,
    )
    return grad, penalty.reshape(SCEN)


def solution(mesh):
    return jax.shard_map(
        body,
        mesh=mesh,
        in_specs=(
            P(None, "bus"),
            P("line", "bus"),
            P("line", "bus"),
            P("bus"),
            P(None, "line"),
            P(),
        ),
        out_specs=(P("line", "bus"), P()),
        check_vma=False,
    )
```

```python
import jax
import jax.numpy as jnp
from jax import lax
from jax.experimental import pallas as pl
from jax.experimental.pallas import tpu as pltpu
from jax.sharding import PartitionSpec as P

LINES = 4096
OUTAGES = 8192
SCEN = 64
BUS_COLS = 2176
ROWS = 512
OUTS = 256
CHUNKS = ((0, 640), (640, 768), (1408, 768))
F32 = jnp.float32
BF16 = jnp.bfloat16
NT = (((1,), (1,)), ((), ()))


def torus(size, step):
    return min(step, size - step)


PLANE = sorted(
    [(dy, dx) for dy in range(4) for dx in range(4) if dy + dx],
    key=lambda step: -torus(4, step[0]) - torus(4, step[1]),
)
COLUMN = sorted(
    [(dz, dc) for dz in range(8) for dc in range(2) if dz + dc], key=lambda step: -torus(8, step[0])
)


def split(value):
    high = value.astype(BF16)
    return high, (value - high.astype(F32)).astype(BF16)


def kernel(
    tier_hbm, inj_hbm, tf_hbm, w_hbm, ol_hbm, table_hbm, grad_ref, pen_ref,
    tier_ref, ol_ref, table_ref,
    tf, tf_hi, tf_lo, inj, inj_hl, w, w_t, w_parts, w_wide, limit_t, lane_hit, spread_in,
    part, s1, s2_src, s2, ol_src, ol_all, s3_src, s3, flow_src, flow_in, lane_of, tile_of,
    flow_t, outage_t, direct_t, back_rows, back_t,
    t1_src, t1, direct_src, direct_in, t2_src, t2, t3_src, t3, pen_src, pen1, pen2_src, pen2,
    r2_src, r2,
    load_sem, send_sem, recv_sem, near_recv, far_back, t3_recv, pair_sem, far_send, far_recv,
):
    i = lax.axis_index("line")
    j = lax.axis_index("bus")
    p = j // 2
    zh = lax.rem(j, 2)
    q = zh * 8 + i
    core = lax.rem(i, 2)
    z = i // 2
    half = lax.rem(p, 2)

    def plane_peer(step):
        other = lax.rem(p // 4 + step[0], 4) * 4 + lax.rem(p + step[1], 4)
        return other, (i, other * 2 + zh)

    def cross_peer(step):
        other, (line, bus) = plane_peer(step)
        return other, (i + 1 - 2 * core, bus)

    def column_peer(step):
        chip = lax.rem(zh * 4 + z + step[0], 8)
        line = lax.rem(chip, 4) * 2 + lax.rem(core + step[1], 2)
        return (chip // 4) * 8 + line, (line, p * 2 + chip // 4)

    barrier = pltpu.get_barrier_semaphore()

    for peer, steps in ((plane_peer, PLANE), (column_peer, COLUMN), (cross_peer, PLANE)):
        for step in steps:
            pl.semaphore_signal(
                barrier, inc=1, device_id=peer(step)[1], device_id_type=pl.DeviceIdType.MESH
            )
    pairs = [(inj_hbm, inj)]
    pairs += [(tf_hbm.at[pl.ds(n * 128, 128)], tf.at[pl.ds(n * 128, 128)]) for n in range(4)]
    pairs += [(ol_hbm, ol_ref), (w_hbm, w), (table_hbm, table_ref), (tier_hbm, tier_ref)]
    loads = [pltpu.make_async_copy(a, b, load_sem.at[n]) for n, (a, b) in enumerate(pairs)]
    for copy in loads:
        copy.start()

    def send_all(peer, phase, source, target, arrived=None, steps=None):
        for step in steps or (PLANE if peer is plane_peer else COLUMN):
            other, device = peer(step)
            pltpu.make_async_remote_copy(
                src_ref=source(other),
                dst_ref=target,
                send_sem=send_sem.at[phase],
                recv_sem=recv_sem.at[phase] if arrived is None else arrived,
                device_id=device,
                device_id_type=pl.DeviceIdType.MESH,
            ).start()

    def arrive_one(semaphore, view):
        pltpu.make_async_copy(view, view, semaphore).wait()

    def arrive(phase, buffer):
        view = buffer.at[pl.ds(0, 15)]
        pltpu.make_async_copy(view, view, recv_sem.at[phase]).wait()

    def sent(phase, buffer):
        view = buffer.at[pl.ds(0, 15)]
        pltpu.make_async_copy(view, view, send_sem.at[phase]).wait()


    loads[0].wait()
    inj_hi, inj_lo = split(inj[...])
    inj_hl[0:SCEN, :] = inj_hi
    inj_hl[SCEN : 2 * SCEN, :] = inj_lo
    for n in range(2):
        for m in (2 * n, 2 * n + 1):
            loads[1 + m].wait()
        high, low = split(tf[n * 256 : (n + 1) * 256, :])
        rows = pl.ds(pl.multiple_of(core * ROWS + n * 256, 256), 256)
        tf_hi[rows, :] = high
        tf_lo[rows, :] = low
        both = lax.dot_general(inj_hl[...], high, NT, preferred_element_type=F32)
        low = lax.dot_general(inj_hl[0:SCEN, :], low, NT, preferred_element_type=F32)
        flows = both[0:SCEN] + (both[SCEN : 2 * SCEN] + low)
        for group in range(8):
            part[2 * group + n] = flows[group * 8 : (group + 1) * 8]

    key_row = lax.broadcasted_iota(jnp.int32, (256, 256), 0)
    key_col = lax.broadcasted_iota(jnp.int32, (256, 256), 1)
    same_half = jnp.bitwise_and(jnp.right_shift(key_row, 5) - jnp.right_shift(key_col, 6), 1) == 0
    key = jnp.where(same_half, jnp.bitwise_and(key_row, 31) - jnp.right_shift(key_col, 7), -1)

    def widen_start():
        w_t[...] = w[...].T

        def group(g, carry):
            piece = w_t[pl.ds(pl.multiple_of(g * 32, 32), 32), :]
            high = piece.astype(BF16).astype(F32)
            rest = piece - high
            middle = rest.astype(BF16).astype(F32)
            stack = [
                value[:, h * 256 : (h + 1) * 256]
                for value in (high, middle, rest - middle)
                for h in range(2)
            ]
            stack.append(jnp.zeros((64, 256), F32))
            w_parts[g] = jnp.concatenate(stack, axis=0).T.astype(BF16)
            return carry

        lax.fori_loop(0, 8, group, 0)

    def widen(step, carry):
        ones = jnp.where(key == 2 * step, 1.0, 0.0).astype(BF16)
        for g in range(8):
            wide = jnp.dot(w_parts[g], ones, preferred_element_type=F32)
            w_wide[g * 32 + 2 * step] = wide[:, 0:128]
            w_wide[g * 32 + 2 * step + 1] = wide[:, 128:256]
        return carry

    pl.semaphore_wait(barrier, 45)
    send_all(plane_peer, 0, lambda other: part.at[other], s1.at[p])
    loads[5].wait()
    ol_src[...] = ol_ref[...].astype(F32)
    send_all(plane_peer, 1, lambda other: ol_src, ol_all.at[p])
    s1[p] = part[p]
    ol_all[p] = ol_src[...]
    for copy in loads[6:]:
        copy.wait()
    tiers = jnp.concatenate([tier_ref[...], tier_ref[...]], axis=1)
    left = lax.broadcasted_iota(jnp.int32, (128, 128), 1) < SCEN
    for block in range(2):
        rows = slice(block * 128, (block + 1) * 128)
        value = jnp.zeros((128, 128), F32)
        for tier in range(4):
            pair = [
                jnp.broadcast_to(
                    0.4 * table_ref[tier : tier + 1, h * 256 + block * 128 : h * 256 + block * 128 + 128].astype(F32),
                    (128, 128),
                ).T
                for h in range(2)
            ]
            value = jnp.where(tiers == tier, jnp.where(left, pair[0], pair[1]), value)
        limit_t[rows, :] = value
    widen_start()
    lax.fori_loop(0, 3, widen, 0)
    arrive(0, s1)
    s2_src[...] = jnp.sum(s1[...], axis=0)
    send_all(column_peer, 2, lambda other: s2_src, s2.at[q], near_recv.at[q])
    s2[q] = s2_src[...]
    arrive(1, ol_all)

    lax.fori_loop(3, 9, widen, 0)
    def names(group, carry):
        where = jnp.broadcast_to(ol_all[group], (8, 256)).astype(jnp.int32)
        lane_of[group] = jnp.bitwise_and(where, 127)
        tile_of[group] = jnp.right_shift(where, 7)
        return carry

    lax.fori_loop(0, 16, names, 0)
    for ahead in (2, 1, 3, 0):
        blocks = [lax.rem(z + ahead, 4) * 2 + c for c in range(2)]
        sources = []
        for block in blocks:
            for h in range(2):
                slot = h * 8 + block

                @pl.when(slot != q)
                def _():
                    arrive_one(near_recv.at[slot], s2.at[slot])

            full = s2[block] + s2[8 + block]
            for k in range(2):
                sources.append((block * 4 + 2 * half + k, full[:, k * 128 : (k + 1) * 128]))
        if ahead == 0:
            flow_src[...] = s2[i] + s2[8 + i]
            send_all(plane_peer, 9, lambda other: flow_src, flow_in.at[p])
        for group in range(16):
            for k in range(2):
                cols = slice(k * 128, (k + 1) * 128)
                lane = lane_of[group, :, cols]
                tile = tile_of[group, :, cols]
                out = jnp.zeros((8, 128), F32) if ahead == 2 else s3_src[group, :, cols]
                for name, source in sources:
                    out = jnp.where(tile == name, jnp.take_along_axis(source, lane, axis=1), out)
                s3_src[group, :, cols] = out
    send_all(plane_peer, 3, lambda other: s3_src.at[other], s3.at[p])
    s3[p] = s3_src[p]
    flow_in[p] = flow_src[...]
    lax.fori_loop(9, 16, widen, 0)
    arrive(3, s3)
    arrive(9, flow_in)
    tiles = jnp.concatenate([flow_in[2 * g + h] for h in range(2) for g in range(8)], axis=0)
    flow_t[...] = tiles.T
    picked = jnp.concatenate([s3[2 * g] + s3[2 * g + 1] for g in range(8)], axis=0)
    outage_t[...] = jnp.concatenate([picked, picked], axis=0).T

    pair = pltpu.make_async_remote_copy(
        src_ref=tf_hbm,
        dst_ref=tf,
        send_sem=pair_sem.at[0],
        recv_sem=pair_sem.at[1],
        device_id=(i + 1 - 2 * core, j),
        device_id_type=pl.DeviceIdType.MESH,
    )
    pair.start()

    penalty = [jnp.zeros((8, 128), F32)] * 4
    for block in range(4):
        slabs = [slice(block * 64 + v * 8, block * 64 + v * 8 + 8) for v in range(8)]
        flow = [flow_t[rows, :] for rows in slabs]
        top = [limit_t[rows, :] for rows in slabs]
        low = [-value for value in top]

        def outages(step, carry):
            direct = list(carry[:8])
            squares = list(carry[8:])
            eight = pl.ds(pl.multiple_of(step * 8, 8), 8)
            near = outage_t[eight, :]
            sums = []
            for u in range(8):
                name = step * 8 + u
                here = jnp.broadcast_to(near[u : u + 1, :], (8, 128))
                back = None
                for v in range(8):
                    factor = w_wide[name, slabs[v], :]
                    post = factor * here + flow[v]
                    over = post - jnp.minimum(jnp.maximum(post, low[v]), top[v])
                    direct[v] = direct[v] + over
                    term = over * factor
                    back = term if back is None else back + term
                    squares[v % 4] = squares[v % 4] + over * over
                if block > 0:
                    back = back + back_rows[name]
                if block < 3:
                    back_rows[name] = back
                else:
                    sums.append(jnp.sum(back, axis=0, keepdims=True))
            if block == 3:
                back_t[eight, :] = jnp.concatenate(sums, axis=0)
            return tuple(direct) + tuple(squares)

        start = tuple(jnp.zeros((8, 128), F32) for _ in range(8)) + tuple(penalty)
        result = lax.fori_loop(0, 32, outages, start)
        for v in range(8):
            direct_t[slabs[v], :] = result[v]
        penalty = result[8:]

    back = back_t[...].T
    back = back[0:SCEN] + back[SCEN : 2 * SCEN]
    for g in range(8):
        t1_src[g] = back[g * 8 : (g + 1) * 8, :]
    send_all(plane_peer, 4, lambda other: t1_src.at[other // 2], t1.at[p], far_back.at[p])
    t1[p] = t1_src[p // 2]
    direct = direct_t[...].T
    for h in range(2):
        for g in range(8):
            direct_src[2 * g + h] = direct[h * SCEN + g * 8 : h * SCEN + g * 8 + 8, :]
    send_all(plane_peer, 10, lambda other: direct_src.at[other], direct_in.at[p])
    direct_in[p] = direct_src[p]
    squares = (penalty[0] + penalty[1]) + (penalty[2] + penalty[3])
    pen_src[...] = jnp.sum(squares, axis=0, keepdims=True)
    send_all(plane_peer, 5, lambda other: pen_src, pen1.at[p])
    pen1[p] = pen_src[...]
    def mark(group, carry):
        lane = jnp.bitwise_and(jnp.broadcast_to(ol_all[group], (128, 256)).astype(jnp.int32), 127)
        hit = lane == lax.broadcasted_iota(jnp.int32, (128, 256), 0)
        lane_hit[group] = jnp.where(hit, 1.0, 0.0).astype(BF16)
        return carry

    lax.fori_loop(0, 16, mark, 0)
    pair.wait()

    def cut(step, carry):
        rows = pl.ds(pl.multiple_of(step * 64, 64), 64)
        high, low = split(tf[rows, :])
        rows = pl.ds(pl.multiple_of((1 - core) * ROWS + step * 64, 64), 64)
        tf_hi[rows, :] = high
        tf_lo[rows, :] = low
        return carry

    lax.fori_loop(0, 8, cut, 0)

    total = jnp.zeros((256, 128), F32)
    for turn, step in enumerate([(0, 0)] + PLANE[::-1]):
        group = plane_peer(step)[0]
        if step != (0, 0):
            arrive_one(far_back.at[group], t1.at[group])
        high, low = split(t1[group])
        both = jnp.concatenate([high.astype(F32), low.astype(F32)], axis=0)
        tile = jnp.concatenate([tile_of[group], tile_of[group]], axis=0) - 2 * half
        for t in range(16):
            name = (t // 2) * 4 + t % 2
            spread_in[turn % 4, t * 16 : (t + 1) * 16, :] = jnp.where(tile == name, both, 0.0).astype(BF16)
        total = total + lax.dot_general(
            spread_in[turn % 4], lane_hit[group], NT, preferred_element_type=F32
        )
    for t in range(16):
        cols = slice((t % 2) * 128, (t % 2) * 128 + 128)
        t2_src[t // 2, :, cols] = total[t * 16 : t * 16 + 8] + total[t * 16 + 8 : t * 16 + 16]
    column = lambda other: t2_src.at[lax.rem(other, 8)]
    send_all(column_peer, 6, column, t2.at[q], steps=[step for step in COLUMN if step != (4, 0)])
    arrive(10, direct_in)
    t2_src[i] = t2_src[i] + jnp.sum(direct_in[...], axis=0)
    send_all(column_peer, 6, column, t2.at[q], steps=[(4, 0)])
    t2[q] = t2_src[i]
    arrive(5, pen1)
    pen2_src[...] = jnp.sum(pen1[...], axis=0)
    send_all(column_peer, 7, lambda other: pen2_src, pen2.at[q])
    pen2[q] = pen2_src[...]
    arrive(6, t2)
    t3_src[...] = jnp.sum(t2[...], axis=0) * (2.0 / OUTAGES)
    target = lax.rem(p // 2, 2)
    slot = core * 8 + (p // 4) * 2 + half

    def hand(step):
        other = plane_peer(step)[0]
        return pltpu.make_async_remote_copy(
            src_ref=t3_src,
            dst_ref=t3.at[slot],
            send_sem=send_sem.at[8],
            recv_sem=t3_recv.at[slot],
            device_id=(z * 2 + target, other * 2 + zh),
            device_id_type=pl.DeviceIdType.MESH,
        )

    for step in PLANE:
        hand(step).start()

    @pl.when(target != core)
    def _():
        hand((0, 0)).start()

    @pl.when(target == core)
    def _():
        t3[slot] = t3_src[...]

    arrive(7, pen2)
    both = jnp.sum(pen2[...], axis=0) * (1.0 / (LINES * OUTAGES))
    pen_ref[...] = both[:, 0:SCEN] + both[:, SCEN:128]
    for n in range(16):

        @pl.when(jnp.logical_or(slot != n, target != core))
        def _():
            arrive_one(t3_recv.at[n], t3.at[n])

    grad = jnp.concatenate(
        [
            jnp.concatenate([t3[c * 8 + a * 2 + h] for a in range(4)], axis=0)
            for c in range(2)
            for h in range(2)
        ],
        axis=1,
    )
    grad_hi, grad_lo = split(grad)
    grad_hl = jnp.concatenate([grad_hi, grad_lo], axis=0)
    right = z // 2
    others = (3 - 3 * right, 2 - right, z + 1 - 2 * lax.rem(z, 2))

    def far_copy(n, d):
        start, width = CHUNKS[n]
        cols = pl.ds(start, width)
        return pltpu.make_async_remote_copy(
            src_ref=r2_src.at[others[d], :, cols],
            dst_ref=r2.at[z, :, cols],
            send_sem=far_send.at[n, d],
            recv_sem=far_recv.at[n, z],
            device_id=(others[d] * 2 + core, j),
            device_id_type=pl.DeviceIdType.MESH,
        )

    for n, (start, width) in enumerate(CHUNKS):
        cols = slice(start, start + width)
        both = jnp.dot(grad_hl, tf_hi[:, cols], preferred_element_type=F32)
        low = jnp.dot(grad_hi, tf_lo[:, cols], preferred_element_type=F32)
        out = both[0:32] + (both[32:64] + low)
        for a in range(4):
            r2_src[a, :, cols] = out[a * 8 : (a + 1) * 8]
        for d in range(2):
            far_copy(n, d).start()
    for n in range(len(CHUNKS)):
        far_copy(n, 2).start()
    r2[z] = r2_src[z]
    for n in range(len(CHUNKS)):
        start, width = CHUNKS[n]
        for d in range(3):
            other = others[2 - d]
            arrive_one(far_recv.at[n, other], r2.at[other, :, pl.ds(start, width)])
            far_copy(n, d).wait_send()
    grad_ref[...] = (r2[0] + r2[1]) + (r2[2] + r2[3])
    for phase, buffer in enumerate((s1, ol_all, s2, s3, t1, pen1, t2, pen2, t3, flow_in, direct_in)):
        sent(phase, buffer)

    @pl.when(target != core)
    def _():
        arrive_one(send_sem.at[8], t3.at[0])


def body(injections, transfer_factors, outage_factors, outage_line, limit_table, scenario_tier):
    tile = (8, 256)
    vmem = pltpu.VMEM
    scratch = [
        vmem((1, SCEN), jnp.int32),
        vmem((1, OUTS), jnp.int32),
        vmem((4, ROWS), jnp.int32),
        vmem((ROWS, BUS_COLS), F32),
        vmem((2 * ROWS, BUS_COLS), BF16),
        vmem((2 * ROWS, BUS_COLS), BF16),
        vmem((SCEN, BUS_COLS), F32),
        vmem((2 * SCEN, BUS_COLS), BF16),
        vmem((ROWS, OUTS), F32),
        vmem((OUTS, ROWS), F32),
        vmem((8, 256, 256), BF16),
        vmem((OUTS, 256, 128), F32),
        vmem((256, 128), F32),
        vmem((16, 128, 256), BF16),
        vmem((4, 256, 256), BF16),
        vmem((16,) + tile, F32),
        vmem((16,) + tile, F32),
        vmem(tile, F32),
        vmem((16,) + tile, F32),
        vmem((1, OUTS), F32),
        vmem((16, 1, OUTS), F32),
        vmem((16,) + tile, F32),
        vmem((16,) + tile, F32),
        vmem(tile, F32),
        vmem((16,) + tile, F32),
        vmem((16,) + tile, jnp.int32),
        vmem((16,) + tile, jnp.int32),
        vmem((256, 128), F32),
        vmem((OUTS, 128), F32),
        vmem((256, 128), F32),
        vmem((OUTS, 8, 128), F32),
        vmem((OUTS, 128), F32),
        vmem((8,) + tile, F32),
        vmem((16,) + tile, F32),
        vmem((16,) + tile, F32),
        vmem((16,) + tile, F32),
        vmem((8,) + tile, F32),
        vmem((16,) + tile, F32),
        vmem(tile, F32),
        vmem((16,) + tile, F32),
        vmem((1, 128), F32),
        vmem((16, 1, 128), F32),
        vmem((1, 128), F32),
        vmem((16, 1, 128), F32),
        vmem((4, 8, BUS_COLS), F32),
        vmem((4, 8, BUS_COLS), F32),
        pltpu.SemaphoreType.DMA((9,)),
        pltpu.SemaphoreType.DMA((11,)),
        pltpu.SemaphoreType.DMA((11,)),
        pltpu.SemaphoreType.DMA((16,)),
        pltpu.SemaphoreType.DMA((16,)),
        pltpu.SemaphoreType.DMA((16,)),
        pltpu.SemaphoreType.DMA((2,)),
        pltpu.SemaphoreType.DMA((3, 3)),
        pltpu.SemaphoreType.DMA((3, 4)),
    ]
    hbm = pl.BlockSpec(memory_space=pl.ANY)
    whole = pl.BlockSpec(memory_space=pltpu.VMEM)
    grad, penalty = pl.pallas_call(
        kernel,
        out_shape=(
            pltpu.VMEM((8, BUS_COLS), F32),
            pltpu.VMEM((1, SCEN), F32),
        ),
        in_specs=[hbm] * 6,
        out_specs=(whole, whole),
        scratch_shapes=scratch,
        compiler_params=pltpu.CompilerParams(
            collective_id=0, has_side_effects=True, vmem_limit_bytes=60 << 20
        ),
        name="overload",
    )(
        scenario_tier.reshape(1, SCEN),
        injections,
        transfer_factors,
        outage_factors,
        outage_line.reshape(1, OUTS),
        limit_table,
    )
    return grad, penalty.reshape(SCEN)


def solution(mesh):
    return jax.shard_map(
        body,
        mesh=mesh,
        in_specs=(
            P(None, "bus"),
            P("line", "bus"),
            P("line", "bus"),
            P("bus"),
            P(None, "line"),
            P(),
        ),
        out_specs=(P("line", "bus"), P()),
        check_vma=False,
    )
```

```python
import jax
import jax.numpy as jnp
from jax import lax
from jax.experimental import pallas as pl
from jax.experimental.pallas import tpu as pltpu
from jax.sharding import PartitionSpec as P

LINES = 4096
OUTAGES = 8192
SCEN = 64
BUS_COLS = 2176
ROWS = 512
OUTS = 256
CHUNKS = ((0, 640), (640, 768), (1408, 768))
F32 = jnp.float32
BF16 = jnp.bfloat16
NT = (((1,), (1,)), ((), ()))


def torus(size, step):
    return min(step, size - step)


PLANE = sorted(
    [(dy, dx) for dy in range(4) for dx in range(4) if dy + dx],
    key=lambda step: -torus(4, step[0]) - torus(4, step[1]),
)
COLUMN = sorted(
    [(dz, dc) for dz in range(8) for dc in range(2) if dz + dc], key=lambda step: -torus(8, step[0])
)


def split(value):
    high = value.astype(BF16)
    return high, (value - high.astype(F32)).astype(BF16)


def kernel(
    tier_hbm, inj_hbm, tf_hbm, w_hbm, ol_hbm, table_hbm, grad_ref, pen_ref,
    tier_ref, ol_ref, table_ref,
    tf, tf_hi, tf_lo, inj, inj_hl, w, w_t, w_parts, w_wide, limit_t, lane_hit, spread_in,
    part, s1, s2_src, s2, ol_src, ol_all, s3_src, s3, flow_src, flow_in, lane_of, tile_of,
    flow_t, outage_t, direct_t, back_rows, back_t,
    t1_src, t1, direct_src, direct_in, t2_src, t2, t3_src, t3, pen_src, pen1, pen2_src, pen2,
    r2_src, r2,
    load_sem, send_sem, recv_sem, near_recv, far_back, t3_recv, pair_sem, far_send, far_recv,
):
    i = lax.axis_index("line")
    j = lax.axis_index("bus")
    p = j // 2
    zh = lax.rem(j, 2)
    q = zh * 8 + i
    core = lax.rem(i, 2)
    z = i // 2
    half = lax.rem(p, 2)

    def plane_peer(step):
        other = lax.rem(p // 4 + step[0], 4) * 4 + lax.rem(p + step[1], 4)
        return other, (i, other * 2 + zh)

    def cross_peer(step):
        other, (line, bus) = plane_peer(step)
        return other, (i + 1 - 2 * core, bus)

    def column_peer(step):
        chip = lax.rem(zh * 4 + z + step[0], 8)
        line = lax.rem(chip, 4) * 2 + lax.rem(core + step[1], 2)
        return (chip // 4) * 8 + line, (line, p * 2 + chip // 4)

    barrier = pltpu.get_barrier_semaphore()

    for peer, steps in ((plane_peer, PLANE), (column_peer, COLUMN), (cross_peer, PLANE)):
        for step in steps:
            pl.semaphore_signal(
                barrier, inc=1, device_id=peer(step)[1], device_id_type=pl.DeviceIdType.MESH
            )
    pairs = [(inj_hbm, inj)]
    pairs += [(tf_hbm.at[pl.ds(n * 128, 128)], tf.at[pl.ds(n * 128, 128)]) for n in range(4)]
    pairs += [(ol_hbm, ol_ref), (w_hbm, w), (table_hbm, table_ref), (tier_hbm, tier_ref)]
    loads = [pltpu.make_async_copy(a, b, load_sem.at[n]) for n, (a, b) in enumerate(pairs)]
    for copy in loads:
        copy.start()

    def send_all(peer, phase, source, target, arrived=None):
        for step in PLANE if peer is plane_peer else COLUMN:
            other, device = peer(step)
            pltpu.make_async_remote_copy(
                src_ref=source(other),
                dst_ref=target,
                send_sem=send_sem.at[phase],
                recv_sem=recv_sem.at[phase] if arrived is None else arrived,
                device_id=device,
                device_id_type=pl.DeviceIdType.MESH,
            ).start()

    def arrive_one(semaphore, view):
        pltpu.make_async_copy(view, view, semaphore).wait()

    def arrive(phase, buffer):
        view = buffer.at[pl.ds(0, 15)]
        pltpu.make_async_copy(view, view, recv_sem.at[phase]).wait()

    def sent(phase, buffer):
        view = buffer.at[pl.ds(0, 15)]
        pltpu.make_async_copy(view, view, send_sem.at[phase]).wait()


    loads[0].wait()
    inj_hi, inj_lo = split(inj[...])
    inj_hl[0:SCEN, :] = inj_hi
    inj_hl[SCEN : 2 * SCEN, :] = inj_lo
    for n in range(2):
        for m in (2 * n, 2 * n + 1):
            loads[1 + m].wait()
        high, low = split(tf[n * 256 : (n + 1) * 256, :])
        rows = pl.ds(pl.multiple_of(core * ROWS + n * 256, 256), 256)
        tf_hi[rows, :] = high
        tf_lo[rows, :] = low
        both = lax.dot_general(inj_hl[...], high, NT, preferred_element_type=F32)
        low = lax.dot_general(inj_hl[0:SCEN, :], low, NT, preferred_element_type=F32)
        flows = both[0:SCEN] + (both[SCEN : 2 * SCEN] + low)
        for group in range(8):
            part[2 * group + n] = flows[group * 8 : (group + 1) * 8]

    key_row = lax.broadcasted_iota(jnp.int32, (256, 256), 0)
    key_col = lax.broadcasted_iota(jnp.int32, (256, 256), 1)
    same_half = jnp.bitwise_and(jnp.right_shift(key_row, 5) - jnp.right_shift(key_col, 6), 1) == 0
    key = jnp.where(same_half, jnp.bitwise_and(key_row, 31) - jnp.right_shift(key_col, 7), -1)

    def widen_start():
        w_t[...] = w[...].T

        def group(g, carry):
            piece = w_t[pl.ds(pl.multiple_of(g * 32, 32), 32), :]
            high = piece.astype(BF16).astype(F32)
            rest = piece - high
            middle = rest.astype(BF16).astype(F32)
            stack = [
                value[:, h * 256 : (h + 1) * 256]
                for value in (high, middle, rest - middle)
                for h in range(2)
            ]
            stack.append(jnp.zeros((64, 256), F32))
            w_parts[g] = jnp.concatenate(stack, axis=0).T.astype(BF16)
            return carry

        lax.fori_loop(0, 8, group, 0)

    def widen(step, carry):
        ones = jnp.where(key == 2 * step, 1.0, 0.0).astype(BF16)
        for g in range(8):
            wide = jnp.dot(w_parts[g], ones, preferred_element_type=F32)
            w_wide[g * 32 + 2 * step] = wide[:, 0:128]
            w_wide[g * 32 + 2 * step + 1] = wide[:, 128:256]
        return carry

    pl.semaphore_wait(barrier, 45)
    send_all(plane_peer, 0, lambda other: part.at[other], s1.at[p])
    loads[5].wait()
    ol_src[...] = ol_ref[...].astype(F32)
    send_all(plane_peer, 1, lambda other: ol_src, ol_all.at[p])
    s1[p] = part[p]
    ol_all[p] = ol_src[...]
    for copy in loads[6:]:
        copy.wait()
    tiers = jnp.concatenate([tier_ref[...], tier_ref[...]], axis=1)
    left = lax.broadcasted_iota(jnp.int32, (128, 128), 1) < SCEN
    for block in range(2):
        rows = slice(block * 128, (block + 1) * 128)
        value = jnp.zeros((128, 128), F32)
        for tier in range(4):
            pair = [
                jnp.broadcast_to(
                    0.4 * table_ref[tier : tier + 1, h * 256 + block * 128 : h * 256 + block * 128 + 128].astype(F32),
                    (128, 128),
                ).T
                for h in range(2)
            ]
            value = jnp.where(tiers == tier, jnp.where(left, pair[0], pair[1]), value)
        limit_t[rows, :] = value
    widen_start()
    lax.fori_loop(0, 3, widen, 0)
    arrive(0, s1)
    s2_src[...] = jnp.sum(s1[...], axis=0)
    send_all(column_peer, 2, lambda other: s2_src, s2.at[q], near_recv.at[q])
    s2[q] = s2_src[...]
    arrive(1, ol_all)

    lax.fori_loop(3, 9, widen, 0)
    def names(group, carry):
        where = jnp.broadcast_to(ol_all[group], (8, 256)).astype(jnp.int32)
        lane_of[group] = jnp.bitwise_and(where, 127)
        tile_of[group] = jnp.right_shift(where, 7)
        return carry

    lax.fori_loop(0, 16, names, 0)
    for ahead in (2, 1, 3, 0):
        blocks = [lax.rem(z + ahead, 4) * 2 + c for c in range(2)]
        sources = []
        for block in blocks:
            for h in range(2):
                slot = h * 8 + block

                @pl.when(slot != q)
                def _():
                    arrive_one(near_recv.at[slot], s2.at[slot])

            full = s2[block] + s2[8 + block]
            for k in range(2):
                sources.append((block * 4 + 2 * half + k, full[:, k * 128 : (k + 1) * 128]))
        for group in range(16):
            for k in range(2):
                cols = slice(k * 128, (k + 1) * 128)
                lane = lane_of[group, :, cols]
                tile = tile_of[group, :, cols]
                out = jnp.zeros((8, 128), F32) if ahead == 2 else s3_src[group, :, cols]
                for name, source in sources:
                    out = jnp.where(tile == name, jnp.take_along_axis(source, lane, axis=1), out)
                s3_src[group, :, cols] = out
    flow_src[...] = s2[i] + s2[8 + i]
    send_all(plane_peer, 3, lambda other: s3_src.at[other], s3.at[p])
    send_all(plane_peer, 9, lambda other: flow_src, flow_in.at[p])
    s3[p] = s3_src[p]
    flow_in[p] = flow_src[...]
    def mark(group, carry):
        lane = jnp.bitwise_and(jnp.broadcast_to(ol_all[group], (128, 256)).astype(jnp.int32), 127)
        hit = lane == lax.broadcasted_iota(jnp.int32, (128, 256), 0)
        lane_hit[group] = jnp.where(hit, 1.0, 0.0).astype(BF16)
        return carry

    lax.fori_loop(0, 16, mark, 0)
    lax.fori_loop(9, 16, widen, 0)
    arrive(3, s3)
    arrive(9, flow_in)
    tiles = jnp.concatenate([flow_in[2 * g + h] for h in range(2) for g in range(8)], axis=0)
    flow_t[...] = tiles.T
    picked = jnp.concatenate([s3[2 * g] + s3[2 * g + 1] for g in range(8)], axis=0)
    outage_t[...] = jnp.concatenate([picked, picked], axis=0).T

    pair = pltpu.make_async_remote_copy(
        src_ref=tf_hbm,
        dst_ref=tf,
        send_sem=pair_sem.at[0],
        recv_sem=pair_sem.at[1],
        device_id=(i + 1 - 2 * core, j),
        device_id_type=pl.DeviceIdType.MESH,
    )
    pair.start()

    penalty = [jnp.zeros((8, 128), F32)] * 4
    for block in range(4):
        slabs = [slice(block * 64 + v * 8, block * 64 + v * 8 + 8) for v in range(8)]
        flow = [flow_t[rows, :] for rows in slabs]
        top = [limit_t[rows, :] for rows in slabs]
        low = [-value for value in top]

        def outages(step, carry):
            direct = list(carry[:8])
            squares = list(carry[8:])
            eight = pl.ds(pl.multiple_of(step * 8, 8), 8)
            near = outage_t[eight, :]
            sums = []
            for u in range(8):
                name = step * 8 + u
                here = jnp.broadcast_to(near[u : u + 1, :], (8, 128))
                back = None
                for v in range(8):
                    factor = w_wide[name, slabs[v], :]
                    post = factor * here + flow[v]
                    over = post - jnp.minimum(jnp.maximum(post, low[v]), top[v])
                    direct[v] = direct[v] + over
                    term = over * factor
                    back = term if back is None else back + term
                    squares[v % 4] = squares[v % 4] + over * over
                if block > 0:
                    back = back + back_rows[name]
                if block < 3:
                    back_rows[name] = back
                else:
                    sums.append(jnp.sum(back, axis=0, keepdims=True))
            if block == 3:
                back_t[eight, :] = jnp.concatenate(sums, axis=0)
            return tuple(direct) + tuple(squares)

        start = tuple(jnp.zeros((8, 128), F32) for _ in range(8)) + tuple(penalty)
        result = lax.fori_loop(0, 32, outages, start)
        for v in range(8):
            direct_t[slabs[v], :] = result[v]
        penalty = result[8:]

    back = back_t[...].T
    back = back[0:SCEN] + back[SCEN : 2 * SCEN]
    for g in range(8):
        t1_src[g] = back[g * 8 : (g + 1) * 8, :]
    send_all(plane_peer, 4, lambda other: t1_src.at[other // 2], t1.at[p], far_back.at[p])
    t1[p] = t1_src[p // 2]
    direct = direct_t[...].T
    for h in range(2):
        for g in range(8):
            direct_src[2 * g + h] = direct[h * SCEN + g * 8 : h * SCEN + g * 8 + 8, :]
    send_all(plane_peer, 10, lambda other: direct_src.at[other], direct_in.at[p])
    direct_in[p] = direct_src[p]
    squares = (penalty[0] + penalty[1]) + (penalty[2] + penalty[3])
    pen_src[...] = jnp.sum(squares, axis=0, keepdims=True)
    send_all(plane_peer, 5, lambda other: pen_src, pen1.at[p])
    pen1[p] = pen_src[...]

    total = jnp.zeros((256, 128), F32)
    for turn, step in enumerate([(0, 0)] + PLANE[::-1]):
        group = plane_peer(step)[0]
        if step != (0, 0):
            arrive_one(far_back.at[group], t1.at[group])
        high, low = split(t1[group])
        both = jnp.concatenate([high.astype(F32), low.astype(F32)], axis=0)
        tile = jnp.concatenate([tile_of[group], tile_of[group]], axis=0) - 2 * half
        for t in range(16):
            name = (t // 2) * 4 + t % 2
            spread_in[turn % 4, t * 16 : (t + 1) * 16, :] = jnp.where(tile == name, both, 0.0).astype(BF16)
        total = total + lax.dot_general(
            spread_in[turn % 4], lane_hit[group], NT, preferred_element_type=F32
        )
    for t in range(16):
        cols = slice((t % 2) * 128, (t % 2) * 128 + 128)
        t2_src[t // 2, :, cols] = total[t * 16 : t * 16 + 8] + total[t * 16 + 8 : t * 16 + 16]
    arrive(10, direct_in)
    t2_src[i] = t2_src[i] + jnp.sum(direct_in[...], axis=0)
    send_all(column_peer, 6, lambda other: t2_src.at[lax.rem(other, 8)], t2.at[q])
    t2[q] = t2_src[i]
    arrive(5, pen1)
    pen2_src[...] = jnp.sum(pen1[...], axis=0)
    send_all(column_peer, 7, lambda other: pen2_src, pen2.at[q])
    pen2[q] = pen2_src[...]
    pair.wait()

    def cut(step, carry):
        rows = pl.ds(pl.multiple_of(step * 64, 64), 64)
        high, low = split(tf[rows, :])
        rows = pl.ds(pl.multiple_of((1 - core) * ROWS + step * 64, 64), 64)
        tf_hi[rows, :] = high
        tf_lo[rows, :] = low
        return carry

    lax.fori_loop(0, 8, cut, 0)
    arrive(6, t2)
    t3_src[...] = jnp.sum(t2[...], axis=0) * (2.0 / OUTAGES)
    target = lax.rem(p // 2, 2)
    slot = core * 8 + (p // 4) * 2 + half

    def hand(step):
        other = plane_peer(step)[0]
        return pltpu.make_async_remote_copy(
            src_ref=t3_src,
            dst_ref=t3.at[slot],
            send_sem=send_sem.at[8],
            recv_sem=t3_recv.at[slot],
            device_id=(z * 2 + target, other * 2 + zh),
            device_id_type=pl.DeviceIdType.MESH,
        )

    for step in PLANE:
        hand(step).start()

    @pl.when(target != core)
    def _():
        hand((0, 0)).start()

    @pl.when(target == core)
    def _():
        t3[slot] = t3_src[...]

    arrive(7, pen2)
    both = jnp.sum(pen2[...], axis=0) * (1.0 / (LINES * OUTAGES))
    pen_ref[...] = both[:, 0:SCEN] + both[:, SCEN:128]
    for n in range(16):

        @pl.when(jnp.logical_or(slot != n, target != core))
        def _():
            arrive_one(t3_recv.at[n], t3.at[n])

    grad = jnp.concatenate(
        [
            jnp.concatenate([t3[c * 8 + a * 2 + h] for a in range(4)], axis=0)
            for c in range(2)
            for h in range(2)
        ],
        axis=1,
    )
    grad_hi, grad_lo = split(grad)
    grad_hl = jnp.concatenate([grad_hi, grad_lo], axis=0)
    right = z // 2
    others = (3 - 3 * right, 2 - right, z + 1 - 2 * lax.rem(z, 2))

    def far_copy(n, d):
        start, width = CHUNKS[n]
        cols = pl.ds(start, width)
        return pltpu.make_async_remote_copy(
            src_ref=r2_src.at[others[d], :, cols],
            dst_ref=r2.at[z, :, cols],
            send_sem=far_send.at[n, d],
            recv_sem=far_recv.at[n, z],
            device_id=(others[d] * 2 + core, j),
            device_id_type=pl.DeviceIdType.MESH,
        )

    for n, (start, width) in enumerate(CHUNKS):
        cols = slice(start, start + width)
        both = jnp.dot(grad_hl, tf_hi[:, cols], preferred_element_type=F32)
        low = jnp.dot(grad_hi, tf_lo[:, cols], preferred_element_type=F32)
        out = both[0:32] + (both[32:64] + low)
        for a in range(4):
            r2_src[a, :, cols] = out[a * 8 : (a + 1) * 8]
        for d in range(2):
            far_copy(n, d).start()
    for n in range(len(CHUNKS)):
        far_copy(n, 2).start()
    r2[z] = r2_src[z]
    for n in range(len(CHUNKS)):
        start, width = CHUNKS[n]
        for d in range(3):
            other = others[2 - d]
            arrive_one(far_recv.at[n, other], r2.at[other, :, pl.ds(start, width)])
            far_copy(n, d).wait_send()
    grad_ref[...] = (r2[0] + r2[1]) + (r2[2] + r2[3])
    for phase, buffer in enumerate((s1, ol_all, s2, s3, t1, pen1, t2, pen2, t3, flow_in, direct_in)):
        sent(phase, buffer)

    @pl.when(target != core)
    def _():
        arrive_one(send_sem.at[8], t3.at[0])


def body(injections, transfer_factors, outage_factors, outage_line, limit_table, scenario_tier):
    tile = (8, 256)
    vmem = pltpu.VMEM
    scratch = [
        vmem((1, SCEN), jnp.int32),
        vmem((1, OUTS), jnp.int32),
        vmem((4, ROWS), jnp.int32),
        vmem((ROWS, BUS_COLS), F32),
        vmem((2 * ROWS, BUS_COLS), BF16),
        vmem((2 * ROWS, BUS_COLS), BF16),
        vmem((SCEN, BUS_COLS), F32),
        vmem((2 * SCEN, BUS_COLS), BF16),
        vmem((ROWS, OUTS), F32),
        vmem((OUTS, ROWS), F32),
        vmem((8, 256, 256), BF16),
        vmem((OUTS, 256, 128), F32),
        vmem((256, 128), F32),
        vmem((16, 128, 256), BF16),
        vmem((4, 256, 256), BF16),
        vmem((16,) + tile, F32),
        vmem((16,) + tile, F32),
        vmem(tile, F32),
        vmem((16,) + tile, F32),
        vmem((1, OUTS), F32),
        vmem((16, 1, OUTS), F32),
        vmem((16,) + tile, F32),
        vmem((16,) + tile, F32),
        vmem(tile, F32),
        vmem((16,) + tile, F32),
        vmem((16,) + tile, jnp.int32),
        vmem((16,) + tile, jnp.int32),
        vmem((256, 128), F32),
        vmem((OUTS, 128), F32),
        vmem((256, 128), F32),
        vmem((OUTS, 8, 128), F32),
        vmem((OUTS, 128), F32),
        vmem((8,) + tile, F32),
        vmem((16,) + tile, F32),
        vmem((16,) + tile, F32),
        vmem((16,) + tile, F32),
        vmem((8,) + tile, F32),
        vmem((16,) + tile, F32),
        vmem(tile, F32),
        vmem((16,) + tile, F32),
        vmem((1, 128), F32),
        vmem((16, 1, 128), F32),
        vmem((1, 128), F32),
        vmem((16, 1, 128), F32),
        vmem((4, 8, BUS_COLS), F32),
        vmem((4, 8, BUS_COLS), F32),
        pltpu.SemaphoreType.DMA((9,)),
        pltpu.SemaphoreType.DMA((11,)),
        pltpu.SemaphoreType.DMA((11,)),
        pltpu.SemaphoreType.DMA((16,)),
        pltpu.SemaphoreType.DMA((16,)),
        pltpu.SemaphoreType.DMA((16,)),
        pltpu.SemaphoreType.DMA((2,)),
        pltpu.SemaphoreType.DMA((3, 3)),
        pltpu.SemaphoreType.DMA((3, 4)),
    ]
    hbm = pl.BlockSpec(memory_space=pl.ANY)
    whole = pl.BlockSpec(memory_space=pltpu.VMEM)
    grad, penalty = pl.pallas_call(
        kernel,
        out_shape=(
            pltpu.VMEM((8, BUS_COLS), F32),
            pltpu.VMEM((1, SCEN), F32),
        ),
        in_specs=[hbm] * 6,
        out_specs=(whole, whole),
        scratch_shapes=scratch,
        compiler_params=pltpu.CompilerParams(
            collective_id=0, has_side_effects=True, vmem_limit_bytes=60 << 20
        ),
        name="overload",
    )(
        scenario_tier.reshape(1, SCEN),
        injections,
        transfer_factors,
        outage_factors,
        outage_line.reshape(1, OUTS),
        limit_table,
    )
    return grad, penalty.reshape(SCEN)


def solution(mesh):
    return jax.shard_map(
        body,
        mesh=mesh,
        in_specs=(
            P(None, "bus"),
            P("line", "bus"),
            P("line", "bus"),
            P("bus"),
            P(None, "line"),
            P(),
        ),
        out_specs=(P("line", "bus"), P()),
        check_vma=False,
    )
```
